32 devices in a mesh: mat: 8 (over z, core), pts: 4 (over y, x).
Axes of the slice: x: 2, y: 2, z: 4, core: 2. Of those that a mesh axis runs over, the one named last changes fastest.
Arguments:
- dens_blocks: bfloat16 [8, 2048, 2048], P(None, 'pts', 'mat'), may hold values from -0.00390625 to 0.00390625
- basis_values: bfloat16 [8, 6144, 1536], P('mat', 'pts'), may hold values from -6 to 6
- kernel: float32 [8, 6144], P('mat', 'pts'), may hold values from 0.3 to 3
- perturbation: float32 [8, 6144], P('mat', 'pts'), may hold values from -6 to 6
- quad_weight: float32 [8, 6144], P('mat', 'pts'), may hold values from 0.002 to 0.02
- point_count: int32 [8, 4], P('mat', 'pts'), may hold values from 192 to 1536, as said below
- active_blocks: int32 [8, 4, 12], P('mat', 'pts'), may hold values from 0 to 15, as said below
- block_pattern: int32 [8, 16, 16], replicated, may hold values 0 or 1
Outputs:
- h_response: float32 [8, 2048, 2048], P(None, 'pts', 'mat')
- n_response: float32 [8, 6144], P('mat', 'pts')
The draws below stay inside these ranges and needn't reach their ends.
Inputs may be any that keep to these rules, and one draw needn't show every extreme that they name: `point_count`: each cluster has at least one shard with exactly 1536 points in use; the others hold 192 or more. `active_blocks`: the 12 entries of one shard are distinct block numbers of its cluster, in no particular order.
All inputs are finite; a program needn't handle non-finite values.
Results may differ from the reference program's by a relative error of at most 0.011.
Values may be sent and summed in bfloat16 or wider, within the bound.
No kernel may reach another device: no remote copies, remote signals or barrier semaphores. Data moves between devices by JAX's collectives and lax.ppermute only.
A program may use at most 128 MiB of HBM per device.

```python
import math
import jax
import jax.numpy as jnp
from jax import lax

BLOCK = 128
ACT = 16
NACT = 12
PTS = 1536
ORB = 2048
NCL = 8
NSHARD = 4
NPTS = 6144


def draw_point_count(key, part):
    key_low = jax.random.fold_in(key, 11)
    key_full = jax.random.fold_in(key, 12)
    counts = jax.random.randint(key_low, (NCL, NSHARD), PTS // 8, PTS + 1, dtype=jnp.int32)
    full_shard = jax.random.randint(key_full, (NCL,), 0, NSHARD, dtype=jnp.int32)
    column = jnp.arange(NSHARD, dtype=jnp.int32)
    return jnp.where(column[None, :] == full_shard[:, None], PTS, counts).astype(jnp.int32)


def draw_active_blocks(key, part):
    subkeys = jax.random.split(jax.random.fold_in(key, 21), NCL * NSHARD)
    orders = jax.vmap(lambda subkey: jax.random.permutation(subkey, ACT))(subkeys)
    return orders[:, :NACT].reshape(NCL, NSHARD, NACT).astype(jnp.int32)


def plant(drawn, key, smallest, top_value):
    place = [jax.random.randint(jax.random.fold_in(key, axis), (), 0, length) for axis, length in enumerate(drawn.shape)]
    longest = drawn.shape.index(max(drawn.shape))
    next_to = place[:longest] + [(place[longest] + 1) % drawn.shape[longest]] + place[longest + 1:]
    return drawn.at[tuple(place)].set(smallest).at[tuple(next_to)].set(top_value)


def shard_levels(own_key, shape, pieces, low, largest):
    loudness, own = 1.0, jax.random.fold_in(own_key, 6)
    for position, blocks in pieces:
        steps = jnp.exp(jax.random.uniform(jax.random.fold_in(own, position), (blocks,), jnp.float32, low / len(pieces), largest / len(pieces)))
        loudness = loudness * jnp.repeat(steps, shape[position] // blocks).reshape([-1 if axis == position else 1 for axis in range(len(shape))])
    return loudness


def scatter_about(stream_key, extent, deviation, most, pieces=(), kind=jnp.bfloat16):
    level = shard_levels(stream_key, extent, pieces, -0.22, 0.18) if pieces else 1.0
    drawn = jax.random.normal(stream_key, extent, jnp.float32) * deviation * level
    return jnp.minimum(jnp.maximum(drawn, -most), most).astype(kind)


def setup_inputs(seed: int = 0) -> dict:
    key_of = jax.random.split(jax.random.key(seed), 9)
    return {
        "dens_blocks": scatter_about(key_of[0], (NCL, ORB, ORB), (NACT * NACT * BLOCK * BLOCK) ** -0.5, 0.00390625, ((1, 4), (2, 8))),
        "basis_values": scatter_about(key_of[1], (NCL, NPTS, NACT * BLOCK), 1.0, 6.0, ((0, 8), (1, 4))),
        "kernel": jnp.clip(jnp.exp(math.log(3.0) - 2.3025851 * jax.random.uniform(key_of[2], (NCL, NPTS), jnp.float32) ** shard_levels(key_of[2], (NCL, NPTS), ((0, 8), (1, 4)), -0.2, 0.2)), 0.3, 3.0),
        "perturbation": scatter_about(key_of[3], (NCL, NPTS), 1.0, 6.0, ((0, 8), (1, 4)), jnp.float32),
        "quad_weight": jnp.clip(jnp.exp(math.log(0.02) - 2.30258502 * jax.random.uniform(key_of[4], (NCL, NPTS), jnp.float32) ** shard_levels(key_of[4], (NCL, NPTS), ((0, 8), (1, 4)), -0.2, 0.2)), 0.002, 0.02),
        "point_count": draw_point_count(jax.random.fold_in(key_of[8], 71), 0),
        "active_blocks": draw_active_blocks(jax.random.fold_in(key_of[8], 71), 0),
        "block_pattern": plant((jax.random.randint(key_of[7], (NCL, ACT, ACT), 0, 4) < 3).astype(jnp.int32), jax.random.fold_in(key_of[7], 1), 0, 1),
    }


def point_block(basis_rows, kernel_rows, perturb_rows, weight_rows, first_point, point_total, submatrix):
    row_count = basis_rows.shape[0]
    inside = (first_point + jnp.arange(row_count, dtype=jnp.int32)) < point_total
    product = jnp.dot(basis_rows, submatrix, preferred_element_type=jnp.float32)
    density = jnp.where(inside, jnp.sum(product * basis_rows.astype(jnp.float32), axis=1), 0.0)
    scaling = jnp.where(inside, weight_rows * (perturb_rows - kernel_rows * density), 0.0)
    scaled = (scaling[:, None] * basis_rows.astype(jnp.float32)).astype(jnp.bfloat16)
    partial_h = jnp.dot(basis_rows.T, scaled, preferred_element_type=jnp.float32)
    return density, partial_h


def reference(dens_blocks, basis_values, kernel, perturbation, quad_weight, point_count, active_blocks, block_pattern):
    def cluster_terms(cluster):
        cluster_density = dens_blocks[cluster]
        cluster_pattern = block_pattern[cluster]
        masked = cluster_density.reshape(ACT, BLOCK, ACT, BLOCK) * cluster_pattern.astype(jnp.bfloat16)[:, None, :, None]

        def shard_step(h_total, shard_id):
            chosen = active_blocks[cluster, shard_id]
            submatrix = masked[chosen][:, :, chosen].reshape(NACT * BLOCK, NACT * BLOCK)
            first_row = shard_id * PTS
            basis_rows = lax.dynamic_slice_in_dim(basis_values[cluster], first_row, PTS, 0)
            kernel_rows = lax.dynamic_slice_in_dim(kernel[cluster], first_row, PTS, 0)
            perturb_rows = lax.dynamic_slice_in_dim(perturbation[cluster], first_row, PTS, 0)
            weight_rows = lax.dynamic_slice_in_dim(quad_weight[cluster], first_row, PTS, 0)
            density, partial_h = point_block(basis_rows, kernel_rows, perturb_rows, weight_rows, 0, point_count[cluster, shard_id], submatrix)
            rounded = lax.optimization_barrier(partial_h.astype(jnp.bfloat16))
            packed = rounded.astype(jnp.float32).reshape(NACT, BLOCK, NACT, BLOCK).transpose(0, 2, 1, 3)
            spread = jnp.zeros((ACT, ACT, BLOCK, BLOCK), jnp.float32).at[chosen[:, None], chosen[None, :]].set(packed)
            return h_total + spread, density

        h_total, densities = lax.scan(shard_step, jnp.zeros((ACT, ACT, BLOCK, BLOCK), jnp.float32), jnp.arange(NSHARD, dtype=jnp.int32))
        mask_full = jnp.repeat(jnp.repeat(cluster_pattern.astype(jnp.float32), BLOCK, axis=0), BLOCK, axis=1)
        h_cluster = h_total.transpose(0, 2, 1, 3).reshape(ORB, ORB) * mask_full
        return h_cluster, densities.reshape(NPTS)

    h_all, n_all = lax.map(cluster_terms, jnp.arange(NCL, dtype=jnp.int32))
    return h_all, n_all
```

```python
import functools

import jax
import jax.numpy as jnp
from jax import lax
from jax.experimental import pallas as pl
from jax.experimental.pallas import tpu as pltpu
from jax.sharding import PartitionSpec as P


BLOCK = 128
VM = pl.BlockSpec(memory_space=pltpu.VMEM)
ANY = pl.BlockSpec(memory_space=pl.ANY)
HEAD = 3


def cost(flops, moved):
    return pl.CostEstimate(flops=int(flops), bytes_accessed=int(moved), transcendentals=0)


def lanes(block):
    return pl.ds(pl.multiple_of(block * BLOCK, BLOCK), BLOCK)


def rows_at(block):
    return pl.ds(pl.multiple_of(block * BLOCK, BLOCK), BLOCK)


def pack_kernel(dims, row, meta, *refs):
    n_mat, n_pts, act, nact = dims
    arrived, packed, stage = refs[:n_mat], refs[n_mat : n_mat + n_pts], refs[-1]
    me_mat, me_pts = meta[0], meta[1]
    width = arrived[0].shape[1]
    for d in range(n_mat):
        m = lax.rem(me_mat - d + n_mat, n_mat)
        stage[:, pl.ds(pl.multiple_of(m * width, BLOCK), width)] = arrived[d][...]
    row_block = me_pts * (act // n_pts) + row
    pattern_at = HEAD + n_pts * nact + row_block * act
    for o in range(n_pts):
        for j in range(nact):
            b = meta[HEAD + o * nact + j]
            keep = meta[pattern_at + b] != 0
            value = stage[:, lanes(b)]
            packed[o][:, j * BLOCK : (j + 1) * BLOCK] = jnp.where(keep, value, jnp.zeros_like(value))


def pack(dims, row, meta, arrived, part):
    n_mat, n_pts, act, nact = dims
    width = arrived[0].shape[1]
    return pl.pallas_call(
        functools.partial(pack_kernel, dims, row),
        out_shape=[jax.ShapeDtypeStruct((BLOCK, nact * BLOCK), jnp.bfloat16)] * n_pts,
        grid_spec=pltpu.PrefetchScalarGridSpec(
            num_scalar_prefetch=1,
            grid=(1,),
            in_specs=[pl.BlockSpec((BLOCK, width), lambda i, meta: (part, 0))] * n_mat,
            out_specs=[pl.BlockSpec((BLOCK, nact * BLOCK), lambda i, meta: (0, 0))] * n_pts,
            scratch_shapes=[pltpu.VMEM((BLOCK, act * BLOCK), jnp.bfloat16)],
        ),
        cost_estimate=cost(0, 2 * BLOCK * BLOCK * (act + n_pts * nact)),
        name=f"pack_{row}",
    )(meta, *arrived)


def invert(dims, meta, place):
    n_mat, n_pts, act, nact = dims
    for a in range(act):
        place[a] = -1
    for i in range(nact):
        place[meta[HEAD + i]] = i


def density_kernel(dims, row, tile, meta, *refs):
    n_mat, n_pts, act, nact = dims
    parts, flipped, before, after, place = refs[:n_pts], refs[n_pts], refs[n_pts + 1], refs[n_pts + 2], refs[n_pts + 3]
    invert(dims, meta, place)
    me_pts = meta[1]
    left = jnp.concatenate([part[...] for part in parts], axis=0)
    points = flipped.shape[1]

    @pl.loop(0, points // tile)
    def _(t):
        at = pl.ds(pl.multiple_of(t * tile, tile), tile)
        inner = jnp.dot(left, flipped[:, at], preferred_element_type=jnp.float32)
        total = before[:, at]
        for o in range(n_pts):
            spot = place[(me_pts ^ o) * (act // n_pts) + row]
            own = flipped[rows_at(jnp.maximum(spot, 0)), at].astype(jnp.float32)
            share = jnp.sum(inner[o * BLOCK : (o + 1) * BLOCK] * own, axis=0, keepdims=True)
            total = total + jnp.where(spot >= 0, share, jnp.zeros_like(share))
        after[:, at] = total


def density(dims, row, meta, parts, flipped, before):
    n_mat, n_pts, act, nact = dims
    orbitals, points = flipped.shape
    return pl.pallas_call(
        functools.partial(density_kernel, dims, row, 256),
        out_shape=jax.ShapeDtypeStruct((1, points), jnp.float32),
        in_specs=[pl.BlockSpec(memory_space=pltpu.SMEM)] + [VM] * (n_pts + 2),
        out_specs=VM,
        scratch_shapes=[pltpu.SMEM((act,), jnp.int32)],
        cost_estimate=cost(2 * n_pts * BLOCK * orbitals * points, 2 * orbitals * points),
        name=f"density_{row}",
    )(meta, *parts, flipped, before)


def response_kernel(dims, row, tile, meta, *refs):
    n_mat, n_pts, act, nact = dims
    flipped, basis, raw, kern, pert, weight = refs[:6]
    out, place, left = refs[6 : 6 + n_pts], refs[-2], refs[-1]
    invert(dims, meta, place)
    me_pts = meta[1]
    points = flipped.shape[1]
    inside = lax.broadcasted_iota(jnp.int32, (1, points), 1) < meta[2]
    n = jnp.where(inside, raw[...], 0.0)
    scaling = jnp.where(inside, weight[...] * (pert[...] - kern[...] * n), 0.0)
    for o in range(n_pts):
        spot = place[(me_pts ^ o) * (act // n_pts) + row]
        own = flipped[rows_at(jnp.maximum(spot, 0)), :].astype(jnp.float32)
        scaled = jnp.where(spot >= 0, own * scaling, 0.0).astype(jnp.bfloat16)
        left[o * BLOCK : (o + 1) * BLOCK, :] = scaled

    @pl.loop(0, basis.shape[1] // tile)
    def _(t):
        at = pl.ds(pl.multiple_of(t * tile, tile), tile)
        block = jnp.dot(left[...], basis[:, at], preferred_element_type=jnp.float32)
        for o in range(n_pts):
            out[o][:, at] = block[o * BLOCK : (o + 1) * BLOCK].astype(jnp.bfloat16)


def response(dims, row, meta, flipped, basis, raw, kern, pert, weight):
    n_mat, n_pts, act, nact = dims
    orbitals, points = flipped.shape
    return pl.pallas_call(
        functools.partial(response_kernel, dims, row, 256),
        out_shape=[jax.ShapeDtypeStruct((BLOCK, orbitals), jnp.bfloat16)] * n_pts,
        in_specs=[pl.BlockSpec(memory_space=pltpu.SMEM)] + [VM] * 6,
        out_specs=[VM] * n_pts,
        scratch_shapes=[
            pltpu.SMEM((act,), jnp.int32),
            pltpu.VMEM((n_pts * BLOCK, points), jnp.bfloat16),
        ],
        cost_estimate=cost(2 * n_pts * BLOCK * orbitals * points, 4 * orbitals * points),
        name=f"response_{row}",
    )(meta, flipped, basis, raw, kern, pert, weight)


def combine_kernel(dims, first, count, meta, *refs):
    n_mat, n_pts, act, nact = dims
    given, out, total = refs[: count * n_pts], refs[count * n_pts : -1], refs[-1]
    me_mat, me_pts = meta[0], meta[1]
    width = act // n_mat * BLOCK
    for r in range(count):
        total[...] = jnp.zeros_like(total)
        for o in range(n_pts):
            part = given[r * n_pts + o]
            for j in range(nact):
                b = meta[HEAD + o * nact + j]
                total[:, lanes(b)] += part[:, j * BLOCK : (j + 1) * BLOCK].astype(jnp.float32)
        row_block = me_pts * (act // n_pts) + first + r
        pattern_at = HEAD + n_pts * nact + row_block * act
        for d in range(n_mat):
            m = lax.rem(me_mat + d, n_mat)
            for k in range(act // n_mat):
                b = m * (act // n_mat) + k
                keep = meta[pattern_at + b] != 0
                value = total[:, lanes(b)]
                value = jnp.where(keep, value, jnp.zeros_like(value))
                out[d][r * BLOCK : (r + 1) * BLOCK, k * BLOCK : (k + 1) * BLOCK] = value.astype(jnp.bfloat16)


def combine(dims, first, count, meta, given):
    n_mat, n_pts, act, nact = dims
    return pl.pallas_call(
        functools.partial(combine_kernel, dims, first, count),
        out_shape=[jax.ShapeDtypeStruct((count * BLOCK, act // n_mat * BLOCK), jnp.bfloat16)] * n_mat,
        in_specs=[pl.BlockSpec(memory_space=pltpu.SMEM)] + [VM] * (count * n_pts),
        out_specs=[VM] * n_mat,
        scratch_shapes=[pltpu.VMEM((BLOCK, act * BLOCK), jnp.float32)],
        cost_estimate=cost(0, 2 * count * BLOCK * BLOCK * (act + n_pts * nact)),
        name=f"combine_{first}",
    )(meta, *given)


def widen_kernel(dims, meta, *refs):
    n_mat = dims[0]
    out = refs[-1]
    for d in range(n_mat):
        c = lax.rem(meta[0] - d + n_mat, n_mat)
        out[c] = refs[d][...].astype(jnp.float32)


def widen(dims, first, count, row_blocks, meta, given, held):
    n_mat = dims[0]
    width = given[0].shape[1]
    shape = jax.ShapeDtypeStruct((n_mat, row_blocks * BLOCK, width), jnp.float32)
    whole = lambda i, meta: (0, 0)
    more = [] if held is None else [held]
    return pl.pallas_call(
        functools.partial(widen_kernel, dims),
        out_shape=shape,
        grid_spec=pltpu.PrefetchScalarGridSpec(
            num_scalar_prefetch=1,
            grid=(1,),
            in_specs=[pl.BlockSpec((count * BLOCK, width), whole)] * n_mat + [ANY] * len(more),
            out_specs=pl.BlockSpec((n_mat, count * BLOCK, width), lambda i, meta: (0, first // count, 0)),
        ),
        input_output_aliases={} if held is None else {1 + n_mat: 0},
        cost_estimate=cost(0, 6 * count * BLOCK * n_mat * width),
        name=f"widen_{first}",
    )(meta, *given, *more)


def split_rows(row_blocks, sizes):
    if sum(sizes) != row_blocks:
        sizes = [1] * row_blocks
    starts = [sum(sizes[:i]) for i in range(len(sizes))]
    return list(zip(starts, sizes))


def body(dens_blocks, basis_values, kernel, perturbation, quad_weight, point_count, active_blocks, block_pattern):
    n_mat, n_pts = lax.axis_size("mat"), lax.axis_size("pts")
    act, nact = block_pattern.shape[1], active_blocks.shape[2]
    dims = (n_mat, n_pts, act, nact)
    row_blocks = act // n_pts
    me_mat, me_pts = lax.axis_index("mat"), lax.axis_index("pts")

    def to_peer(value, o):
        return lax.ppermute(value, "pts", [(i, i ^ o) for i in range(n_pts)])

    def around(value, d):
        return lax.ppermute(value, "mat", [(i, (i + d) % n_mat) for i in range(n_mat)])

    own_active = active_blocks[0, 0]
    peers = [own_active] + [to_peer(own_active, o) for o in range(1, n_pts)]
    pattern = lax.dynamic_index_in_dim(block_pattern, me_mat, 0, keepdims=False).reshape(-1)
    head = jnp.stack([me_mat, me_pts, point_count[0, 0]]).astype(jnp.int32)
    meta = jnp.concatenate([head] + peers + [pattern])

    basis = basis_values[0]
    flipped = basis.T

    raw = jnp.zeros((1, basis.shape[0]), jnp.float32)
    for first, count in split_rows(row_blocks, [1, 1, 2]):
        arrived = []
        for d in range(n_mat):
            piece = lax.dynamic_slice(
                dens_blocks,
                (lax.rem(me_mat + d, n_mat), first * BLOCK, 0),
                (1, count * BLOCK, dens_blocks.shape[2]),
            )[0]
            arrived.append(around(piece, d) if d else piece)
        for part in range(count):
            packed = pack(dims, first + part, meta, arrived, part)
            parts = [packed[0]] + [to_peer(packed[o], o) for o in range(1, n_pts)]
            raw = density(dims, first + part, meta, parts, flipped, raw)

    points = basis.shape[0]
    inside = jnp.arange(points, dtype=jnp.int32)[None, :] < point_count[0, 0]
    n_response = jnp.where(inside, raw, 0.0)

    held = None
    for first, count in split_rows(row_blocks, [2, 1, 1]):
        given = []
        for part in range(count):
            sent = response(dims, first + part, meta, flipped, basis, raw, kernel, perturbation, quad_weight)
            given += [sent[0]] + [to_peer(sent[o], o) for o in range(1, n_pts)]
        cut = combine(dims, first, count, meta, given)
        back = [cut[0]] + [around(cut[d], d) for d in range(1, n_mat)]
        held = widen(dims, first, count, row_blocks, meta, back, held)
    return held, n_response


def solution(mesh):
    placed = (
        P(None, "pts", "mat"),
        P("mat", "pts", None),
        P("mat", "pts"),
        P("mat", "pts"),
        P("mat", "pts"),
        P("mat", "pts"),
        P("mat", "pts", None),
        P(),
    )
    return jax.shard_map(
        body,
        mesh=mesh,
        in_specs=placed,
        out_specs=(P(None, "pts", "mat"), P("mat", "pts")),
        check_vma=False,
    )
```

```python
import functools

import jax
import jax.numpy as jnp
from jax import lax
from jax.experimental import pallas as pl
from jax.experimental.pallas import tpu as pltpu
from jax.sharding import PartitionSpec as P


BLOCK = 128
VM = pl.BlockSpec(memory_space=pltpu.VMEM)
ANY = pl.BlockSpec(memory_space=pl.ANY)
HEAD = 3
GRANT = pltpu.CompilerParams(vmem_limit_bytes=20 << 20)


def cost(flops, moved):
    return pl.CostEstimate(flops=int(flops), bytes_accessed=int(moved), transcendentals=0)


def lanes(block):
    return pl.ds(pl.multiple_of(block * BLOCK, BLOCK), BLOCK)


def rows_at(block):
    return pl.ds(pl.multiple_of(block * BLOCK, BLOCK), BLOCK)


def pack_kernel(dims, row, meta, *refs):
    n_mat, n_pts, act, nact = dims
    arrived, packed, stage = refs[:n_mat], refs[n_mat : n_mat + n_pts], refs[-1]
    me_mat, me_pts = meta[0], meta[1]
    width = arrived[0].shape[1]
    for d in range(n_mat):
        m = lax.rem(me_mat - d + n_mat, n_mat)
        stage[:, pl.ds(pl.multiple_of(m * width, BLOCK), width)] = arrived[d][...]
    row_block = me_pts * (act // n_pts) + row
    pattern_at = HEAD + n_pts * nact + row_block * act
    for o in range(n_pts):
        for j in range(nact):
            b = meta[HEAD + o * nact + j]
            keep = meta[pattern_at + b] != 0
            value = stage[:, lanes(b)]
            packed[o][:, j * BLOCK : (j + 1) * BLOCK] = jnp.where(keep, value, jnp.zeros_like(value))


def pack(dims, row, meta, arrived, part):
    n_mat, n_pts, act, nact = dims
    width = arrived[0].shape[1]
    return pl.pallas_call(
        functools.partial(pack_kernel, dims, row),
        out_shape=[jax.ShapeDtypeStruct((BLOCK, nact * BLOCK), jnp.bfloat16)] * n_pts,
        grid_spec=pltpu.PrefetchScalarGridSpec(
            num_scalar_prefetch=1,
            grid=(1,),
            in_specs=[pl.BlockSpec((BLOCK, width), lambda i, meta: (part, 0))] * n_mat,
            out_specs=[pl.BlockSpec((BLOCK, nact * BLOCK), lambda i, meta: (0, 0))] * n_pts,
            scratch_shapes=[pltpu.VMEM((BLOCK, act * BLOCK), jnp.bfloat16)],
        ),
        compiler_params=GRANT,
        cost_estimate=cost(0, 2 * BLOCK * BLOCK * (act + n_pts * nact)),
    )(meta, *arrived)


def transpose_kernel(given, out):
    out[...] = given[...].T


def transposed(basis):
    points, orbitals = basis.shape
    tile = 256
    return pl.pallas_call(
        transpose_kernel,
        out_shape=jax.ShapeDtypeStruct((orbitals, points), basis.dtype),
        grid=(points // tile,),
        in_specs=[pl.BlockSpec((tile, orbitals), lambda i: (i, 0))],
        out_specs=pl.BlockSpec((orbitals, tile), lambda i: (0, i)),
        compiler_params=GRANT,
        cost_estimate=cost(0, 4 * points * orbitals),
        name="flip",
    )(basis)


def invert(dims, meta, place):
    _, _, act, nact = dims
    for a in range(act):
        place[a] = -1
    for i in range(nact):
        place[meta[HEAD + i]] = i


def density_kernel(dims, row, tile, meta, *refs):
    _, n_pts, act, _ = dims
    parts, flipped, before, after, place = refs[:n_pts], refs[n_pts], refs[n_pts + 1], refs[n_pts + 2], refs[n_pts + 3]
    invert(dims, meta, place)
    me_pts = meta[1]
    left = jnp.concatenate([part[...] for part in parts], axis=0)
    points = flipped.shape[1]

    @pl.loop(0, points // tile)
    def _(t):
        at = pl.ds(pl.multiple_of(t * tile, tile), tile)
        inner = jnp.dot(left, flipped[:, at], preferred_element_type=jnp.float32)
        total = before[:, at]
        for o in range(n_pts):
            spot = place[(me_pts ^ o) * (act // n_pts) + row]
            own = flipped[rows_at(jnp.maximum(spot, 0)), at].astype(jnp.float32)
            share = jnp.sum(inner[o * BLOCK : (o + 1) * BLOCK] * own, axis=0, keepdims=True)
            total = total + jnp.where(spot >= 0, share, jnp.zeros_like(share))
        after[:, at] = total


def density(dims, row, meta, parts, flipped, before):
    _, n_pts, act, _ = dims
    orbitals, points = flipped.shape
    return pl.pallas_call(
        functools.partial(density_kernel, dims, row, 256),
        out_shape=jax.ShapeDtypeStruct((1, points), jnp.float32),
        in_specs=[pl.BlockSpec(memory_space=pltpu.SMEM)] + [VM] * (n_pts + 2),
        out_specs=VM,
        scratch_shapes=[pltpu.SMEM((act,), jnp.int32)],
        compiler_params=GRANT,
        cost_estimate=cost(2 * n_pts * BLOCK * orbitals * points, 2 * orbitals * points),
    )(meta, *parts, flipped, before)


def response_kernel(dims, row, tile, meta, *refs):
    _, n_pts, act, _ = dims
    flipped, basis, raw, kern, pert, weight = refs[:6]
    out, place, left = refs[6 : 6 + n_pts], refs[-2], refs[-1]
    invert(dims, meta, place)
    me_pts = meta[1]
    points = flipped.shape[1]
    inside = lax.broadcasted_iota(jnp.int32, (1, points), 1) < meta[2]
    n = jnp.where(inside, raw[...], 0.0)
    scaling = jnp.where(inside, weight[...] * (pert[...] - kern[...] * n), 0.0)
    for o in range(n_pts):
        spot = place[(me_pts ^ o) * (act // n_pts) + row]
        own = flipped[rows_at(jnp.maximum(spot, 0)), :].astype(jnp.float32)
        scaled = jnp.where(spot >= 0, own * scaling, 0.0).astype(jnp.bfloat16)
        left[o * BLOCK : (o + 1) * BLOCK, :] = scaled

    @pl.loop(0, basis.shape[1] // tile)
    def _(t):
        at = pl.ds(pl.multiple_of(t * tile, tile), tile)
        block = jnp.dot(left[...], basis[:, at], preferred_element_type=jnp.float32)
        for o in range(n_pts):
            out[o][:, at] = block[o * BLOCK : (o + 1) * BLOCK].astype(jnp.bfloat16)


def response(dims, row, meta, flipped, basis, raw, kern, pert, weight):
    _, n_pts, act, _ = dims
    orbitals, points = flipped.shape
    return pl.pallas_call(
        functools.partial(response_kernel, dims, row, 256),
        out_shape=[jax.ShapeDtypeStruct((BLOCK, orbitals), jnp.bfloat16)] * n_pts,
        in_specs=[pl.BlockSpec(memory_space=pltpu.SMEM)] + [VM] * 6,
        out_specs=[VM] * n_pts,
        scratch_shapes=[
            pltpu.SMEM((act,), jnp.int32),
            pltpu.VMEM((n_pts * BLOCK, points), jnp.bfloat16),
        ],
        compiler_params=GRANT,
        cost_estimate=cost(2 * n_pts * BLOCK * orbitals * points, 4 * orbitals * points),
    )(meta, flipped, basis, raw, kern, pert, weight)


def combine_kernel(dims, first, count, meta, *refs):
    n_mat, n_pts, act, nact = dims
    given, out, total = refs[: count * n_pts], refs[count * n_pts : -1], refs[-1]
    me_mat, me_pts = meta[0], meta[1]
    for r in range(count):
        total[...] = jnp.zeros_like(total)
        for o in range(n_pts):
            part = given[r * n_pts + o]
            for j in range(nact):
                b = meta[HEAD + o * nact + j]
                total[:, lanes(b)] += part[:, j * BLOCK : (j + 1) * BLOCK].astype(jnp.float32)
        row_block = me_pts * (act // n_pts) + first + r
        pattern_at = HEAD + n_pts * nact + row_block * act
        for d in range(n_mat):
            m = lax.rem(me_mat + d, n_mat)
            for k in range(act // n_mat):
                b = m * (act // n_mat) + k
                keep = meta[pattern_at + b] != 0
                value = total[:, lanes(b)]
                value = jnp.where(keep, value, jnp.zeros_like(value))
                out[d][r * BLOCK : (r + 1) * BLOCK, k * BLOCK : (k + 1) * BLOCK] = value.astype(jnp.bfloat16)


def combine(dims, first, count, meta, given):
    n_mat, n_pts, act, nact = dims
    return pl.pallas_call(
        functools.partial(combine_kernel, dims, first, count),
        out_shape=[jax.ShapeDtypeStruct((count * BLOCK, act // n_mat * BLOCK), jnp.bfloat16)] * n_mat,
        in_specs=[pl.BlockSpec(memory_space=pltpu.SMEM)] + [VM] * (count * n_pts),
        out_specs=[VM] * n_mat,
        scratch_shapes=[pltpu.VMEM((BLOCK, act * BLOCK), jnp.float32)],
        compiler_params=GRANT,
        cost_estimate=cost(0, 2 * count * BLOCK * BLOCK * (act + n_pts * nact)),
    )(meta, *given)


def widen_kernel(dims, meta, *refs):
    n_mat = dims[0]
    out = refs[-1]
    for d in range(n_mat):
        c = lax.rem(meta[0] - d + n_mat, n_mat)
        out[c] = refs[d][...].astype(jnp.float32)


def widen(dims, first, count, row_blocks, meta, given, held):
    n_mat = dims[0]
    width = given[0].shape[1]
    shape = jax.ShapeDtypeStruct((n_mat, row_blocks * BLOCK, width), jnp.float32)
    whole = lambda i, meta: (0, 0)
    more = [] if held is None else [held]
    return pl.pallas_call(
        functools.partial(widen_kernel, dims),
        out_shape=shape,
        grid_spec=pltpu.PrefetchScalarGridSpec(
            num_scalar_prefetch=1,
            grid=(1,),
            in_specs=[pl.BlockSpec((count * BLOCK, width), whole)] * n_mat + [ANY] * len(more),
            out_specs=pl.BlockSpec((n_mat, count * BLOCK, width), lambda i, meta: (0, first // count, 0)),
        ),
        input_output_aliases={} if held is None else {1 + n_mat: 0},
        compiler_params=GRANT,
        cost_estimate=cost(0, 6 * count * BLOCK * n_mat * width),
    )(meta, *given, *more)


def split_rows(row_blocks, sizes):
    if sum(sizes) != row_blocks:
        sizes = [1] * row_blocks
    starts = [sum(sizes[:i]) for i in range(len(sizes))]
    return list(zip(starts, sizes))


def body(dens_blocks, basis_values, kernel, perturbation, quad_weight, point_count, active_blocks, block_pattern):
    n_mat, n_pts = lax.axis_size("mat"), lax.axis_size("pts")
    act, nact = block_pattern.shape[1], active_blocks.shape[2]
    dims = (n_mat, n_pts, act, nact)
    row_blocks = act // n_pts
    me_mat, me_pts = lax.axis_index("mat"), lax.axis_index("pts")

    def to_peer(value, o):
        return lax.ppermute(value, "pts", [(i, i ^ o) for i in range(n_pts)])

    def around(value, d):
        return lax.ppermute(value, "mat", [(i, (i + d) % n_mat) for i in range(n_mat)])

    points = basis_values.shape[1]
    basis = basis_values[0]
    own_active = active_blocks[0, 0]

    chunks_in = split_rows(row_blocks, [1, 1, 2])
    pieces = {}
    for first, count in chunks_in:
        pieces[first] = [
            lax.dynamic_slice(
                dens_blocks,
                (lax.rem(me_mat + d, n_mat), first * BLOCK, 0),
                (1, count * BLOCK, dens_blocks.shape[2]),
            )[0]
            for d in range(n_mat)
        ]
    arrived = {}

    def fetch(first):
        arrived[first] = [around(piece, d) if d else piece for d, piece in enumerate(pieces[first])]

    parts = {}

    def spread(first, part):
        row = first + part
        packed = pack(dims, row, meta, arrived[first], part)
        parts[row] = [packed[0]] + [to_peer(packed[o], o) for o in range(1, n_pts)]

    fetch(chunks_in[0][0])
    peers = [own_active] + [to_peer(own_active, o) for o in range(1, n_pts)]
    pattern = lax.dynamic_index_in_dim(block_pattern, me_mat, 0, keepdims=False).reshape(-1)
    head = jnp.stack([me_mat, me_pts, point_count[0, 0]]).astype(jnp.int32)
    meta = jnp.concatenate([head] + peers + [pattern])

    order = [(first, part) for first, count in chunks_in for part in range(count)]
    ahead = [first for first, count in chunks_in[1:]]
    for at, (first, part) in enumerate(order):
        spread(first, part)
        if at == 0:
            for later in ahead:
                fetch(later)
        if at == min(1, len(order) - 1):
            flipped = transposed(basis)

    raw = jnp.zeros((1, points), jnp.float32)
    for row in range(row_blocks):
        raw = density(dims, row, meta, parts[row], flipped, raw)

    inside = jnp.arange(points, dtype=jnp.int32)[None, :] < point_count[0, 0]
    n_response = jnp.where(inside, raw, 0.0)

    given = {}
    for row in range(row_blocks):
        sent = response(dims, row, meta, flipped, basis, raw, kernel, perturbation, quad_weight)
        given[row] = [sent[0]] + [to_peer(sent[o], o) for o in range(1, n_pts)]

    chunks_out = split_rows(row_blocks, [2, 1, 1])
    back = {}
    for first, count in chunks_out:
        cut = combine(dims, first, count, meta, sum([given[first + r] for r in range(count)], []))
        back[first] = [cut[0]] + [around(cut[d], d) for d in range(1, n_mat)]
    held = None
    for first, count in chunks_out:
        held = widen(dims, first, count, row_blocks, meta, back[first], held)
    return held, n_response


def solution(mesh):
    placed = (
        P(None, "pts", "mat"),
        P("mat", "pts", None),
        P("mat", "pts"),
        P("mat", "pts"),
        P("mat", "pts"),
        P("mat", "pts"),
        P("mat", "pts", None),
        P(),
    )

    return jax.shard_map(
        body,
        mesh=mesh,
        in_specs=placed,
        out_specs=(P(None, "pts", "mat"), P("mat", "pts")),
        check_vma=False,
    )
```

```python
import functools

import jax
import jax.numpy as jnp
from jax import lax
from jax.experimental import pallas as pl
from jax.experimental.pallas import tpu as pltpu
from jax.sharding import PartitionSpec as P


BLOCK = 128
VM = pl.BlockSpec(memory_space=pltpu.VMEM)
ANY = pl.BlockSpec(memory_space=pl.ANY)
HEAD = 3
GRANT = pltpu.CompilerParams(vmem_limit_bytes=20 << 20)


def cost(flops, moved):
    return pl.CostEstimate(flops=int(flops), bytes_accessed=int(moved), transcendentals=0)


def lanes(block):
    return pl.ds(pl.multiple_of(block * BLOCK, BLOCK), BLOCK)


def pack_kernel(dims, start, single, meta, *refs):
    n_mat, n_pts, act, nact = dims
    each = act // n_mat
    if single:
        arrived, packed = refs[0], refs[1:]
    else:
        packed, stage = refs[n_mat:-1], refs[-1]
        for d in range(n_mat):
            stage[meta[0] ^ d] = refs[d][...]
        arrived = stage
    row_block = meta[1] * (act // n_pts) + start // BLOCK
    pattern_at = HEAD + n_pts * nact + row_block * act
    for o in range(n_pts):
        for j in range(nact):
            b = meta[HEAD + o * nact + j]
            keep = meta[pattern_at + b] != 0
            value = arrived[b // each, :, lanes(lax.rem(b, each))]
            packed[o][:, j * BLOCK : (j + 1) * BLOCK] = jnp.where(keep, value, jnp.zeros_like(value))


def pack(dims, start, rows, meta, arrived, skip):
    n_mat, n_pts, act, nact = dims
    single = not isinstance(arrived, list)
    width = act // n_mat * BLOCK
    if single:
        given = [pl.BlockSpec((n_mat, rows, width), lambda i, meta: (0, skip // rows, 0))]
        scratch = []
    else:
        given = [pl.BlockSpec((rows, width), lambda i, meta: (skip // rows, 0))] * n_mat
        scratch = [pltpu.VMEM((n_mat, rows, width), jnp.bfloat16)]
    return pl.pallas_call(
        functools.partial(pack_kernel, dims, start, single),
        out_shape=[jax.ShapeDtypeStruct((rows, nact * BLOCK), jnp.bfloat16)] * n_pts,
        grid_spec=pltpu.PrefetchScalarGridSpec(
            num_scalar_prefetch=1,
            grid=(1,),
            in_specs=given,
            out_specs=[pl.BlockSpec((rows, nact * BLOCK), lambda i, meta: (0, 0))] * n_pts,
            scratch_shapes=scratch,
        ),
        compiler_params=GRANT,
        cost_estimate=cost(0, 2 * rows * BLOCK * (act + n_pts * nact)),
    )(meta, *([arrived] if single else arrived))


def transpose_kernel(given, out):
    out[...] = given[...].T


def transposed(basis):
    points, orbitals = basis.shape
    tile = 256
    return pl.pallas_call(
        transpose_kernel,
        out_shape=jax.ShapeDtypeStruct((orbitals, points), basis.dtype),
        grid=(points // tile,),
        in_specs=[pl.BlockSpec((tile, orbitals), lambda i: (i, 0))],
        out_specs=pl.BlockSpec((orbitals, tile), lambda i: (0, i)),
        compiler_params=GRANT,
        cost_estimate=cost(0, 4 * points * orbitals),
        name="flip",
    )(basis)


def invert(dims, meta, place):
    _, _, act, nact = dims
    for a in range(act):
        place[a] = -1
    for i in range(nact):
        place[meta[HEAD + i]] = i


def rows_of(place, block, start, rows):
    spot = place[block]
    at = jnp.maximum(spot, 0) * BLOCK + start % BLOCK
    return pl.ds(pl.multiple_of(at, rows), rows), spot >= 0


def density_kernel(dims, start, rows, tile, meta, *refs):
    _, n_pts, act, _ = dims
    parts, flipped, before, after, place = refs[:n_pts], refs[n_pts], refs[n_pts + 1], refs[n_pts + 2], refs[n_pts + 3]
    invert(dims, meta, place)
    left = jnp.concatenate([part[...] for part in parts], axis=0)
    points = flipped.shape[1]

    @pl.loop(0, points // tile)
    def _(t):
        at = pl.ds(pl.multiple_of(t * tile, tile), tile)
        inner = jnp.dot(left, flipped[:, at], preferred_element_type=jnp.float32)
        total = before[:, at]
        for o in range(n_pts):
            where, active = rows_of(place, (meta[1] ^ o) * (act // n_pts) + start // BLOCK, start, rows)
            own = flipped[where, at].astype(jnp.float32)
            share = jnp.sum(inner[o * rows : (o + 1) * rows] * own, axis=0, keepdims=True)
            total = total + jnp.where(active, share, jnp.zeros_like(share))
        after[:, at] = total


def density(dims, start, rows, meta, parts, flipped, before):
    _, n_pts, act, _ = dims
    orbitals, points = flipped.shape
    return pl.pallas_call(
        functools.partial(density_kernel, dims, start, rows, 256),
        out_shape=jax.ShapeDtypeStruct((1, points), jnp.float32),
        in_specs=[pl.BlockSpec(memory_space=pltpu.SMEM)] + [VM] * (n_pts + 2),
        out_specs=VM,
        scratch_shapes=[pltpu.SMEM((act,), jnp.int32)],
        compiler_params=GRANT,
        cost_estimate=cost(2 * n_pts * rows * orbitals * points, 2 * orbitals * points),
    )(meta, *parts, flipped, before)


def response_kernel(dims, start, rows, tile, meta, *refs):
    _, n_pts, act, _ = dims
    flipped, basis, raw, kern, pert, weight = refs[:6]
    out, place, left = refs[6 : 6 + n_pts], refs[-2], refs[-1]
    invert(dims, meta, place)
    points = flipped.shape[1]
    inside = lax.broadcasted_iota(jnp.int32, (1, points), 1) < meta[2]
    n = jnp.where(inside, raw[...], 0.0)
    scaling = jnp.where(inside, weight[...] * (pert[...] - kern[...] * n), 0.0)
    for o in range(n_pts):
        where, active = rows_of(place, (meta[1] ^ o) * (act // n_pts) + start // BLOCK, start, rows)
        own = flipped[where, :].astype(jnp.float32)
        left[o * rows : (o + 1) * rows, :] = jnp.where(active, own * scaling, 0.0).astype(jnp.bfloat16)

    @pl.loop(0, basis.shape[1] // tile)
    def _(t):
        at = pl.ds(pl.multiple_of(t * tile, tile), tile)
        block = jnp.dot(left[...], basis[:, at], preferred_element_type=jnp.float32)
        for o in range(n_pts):
            out[o][:, at] = block[o * rows : (o + 1) * rows].astype(jnp.bfloat16)


def response(dims, start, rows, meta, flipped, basis, raw, kern, pert, weight):
    _, n_pts, act, _ = dims
    orbitals, points = flipped.shape
    return pl.pallas_call(
        functools.partial(response_kernel, dims, start, rows, 256),
        out_shape=[jax.ShapeDtypeStruct((rows, orbitals), jnp.bfloat16)] * n_pts,
        in_specs=[pl.BlockSpec(memory_space=pltpu.SMEM)] + [VM] * 6,
        out_specs=[VM] * n_pts,
        scratch_shapes=[
            pltpu.SMEM((act,), jnp.int32),
            pltpu.VMEM((n_pts * rows, points), jnp.bfloat16),
        ],
        compiler_params=GRANT,
        cost_estimate=cost(2 * n_pts * rows * orbitals * points, 4 * orbitals * points),
    )(meta, flipped, basis, raw, kern, pert, weight)


def combine_kernel(dims, strips, single, meta, *refs):
    n_mat, n_pts, act, nact = dims
    given = len(strips) * n_pts
    out, total = refs[given:-1], refs[-1]
    each = act // n_mat
    done = 0
    for s, (start, rows) in enumerate(strips):
        total[...] = jnp.zeros_like(total)
        for o in range(n_pts):
            part = refs[s * n_pts + o]
            for j in range(nact):
                b = meta[HEAD + o * nact + j]
                total[:rows, lanes(b)] += part[:, j * BLOCK : (j + 1) * BLOCK].astype(jnp.float32)
        row_block = meta[1] * (act // n_pts) + start // BLOCK
        pattern_at = HEAD + n_pts * nact + row_block * act
        for d in range(n_mat):
            m = d if single else meta[0] ^ d
            for k in range(each):
                b = m * each + k
                keep = meta[pattern_at + b] != 0
                value = total[:rows, lanes(b)]
                value = jnp.where(keep, value, jnp.zeros_like(value)).astype(jnp.bfloat16)
                to = out[0].at[d] if single else out[d]
                to[done : done + rows, k * BLOCK : (k + 1) * BLOCK] = value
        done += rows


def combine(dims, strips, single, meta, given):
    n_mat, n_pts, act, nact = dims
    rows = sum(rows for start, rows in strips)
    width = act // n_mat * BLOCK
    if single:
        shapes = [jax.ShapeDtypeStruct((n_mat, rows, width), jnp.bfloat16)]
    else:
        shapes = [jax.ShapeDtypeStruct((rows, width), jnp.bfloat16)] * n_mat
    return pl.pallas_call(
        functools.partial(combine_kernel, dims, strips, single),
        out_shape=shapes,
        in_specs=[pl.BlockSpec(memory_space=pltpu.SMEM)] + [VM] * len(given),
        out_specs=[VM] * len(shapes),
        scratch_shapes=[pltpu.VMEM((BLOCK, act * BLOCK), jnp.float32)],
        compiler_params=GRANT,
        cost_estimate=cost(0, 2 * rows * BLOCK * (act + n_pts * nact)),
    )(meta, *given)


def widen_kernel(single, n_mat, meta, *refs):
    out = refs[-1]
    if single:
        out[...] = refs[0][...].astype(jnp.float32)
    else:
        for d in range(n_mat):
            out[meta[0] ^ d] = refs[d][...].astype(jnp.float32)


def widen(dims, start, rows, all_rows, meta, given, held):
    n_mat, _, act, _ = dims
    single = not isinstance(given, list)
    width = act // n_mat * BLOCK
    if single:
        specs, given = [pl.BlockSpec((n_mat, rows, width), lambda i, meta: (0, 0, 0))], [given]
    else:
        specs = [pl.BlockSpec((rows, width), lambda i, meta: (0, 0))] * n_mat
    more = [] if held is None else [held]
    return pl.pallas_call(
        functools.partial(widen_kernel, single, n_mat),
        out_shape=jax.ShapeDtypeStruct((n_mat, all_rows, width), jnp.float32),
        grid_spec=pltpu.PrefetchScalarGridSpec(
            num_scalar_prefetch=1,
            grid=(1,),
            in_specs=specs + [ANY] * len(more),
            out_specs=pl.BlockSpec((n_mat, rows, width), lambda i, meta: (0, start // rows, 0)),
        ),
        input_output_aliases={} if held is None else {1 + len(given): 0},
        compiler_params=GRANT,
        cost_estimate=cost(0, 6 * rows * n_mat * width),
    )(meta, *given, *more)


def chunks(row_blocks, shape):
    half = BLOCK // 2
    if sum(sum(sizes) for single, sizes in shape) != 2 * row_blocks:
        shape = [(False, [2])] * row_blocks
    out, at = [], 0
    for single, sizes in shape:
        strips = []
        for size in sizes:
            strips.append((at, size * half))
            at += size * half
        out.append((single, tuple(strips)))
    return out


def plan_of(row_blocks):
    inward = chunks(row_blocks, [(False, [2]), (False, [2]), (True, [2, 1, 1])])
    outward = chunks(row_blocks, [(True, [1, 1]), (True, [2]), (True, [2]), (False, [1]), (False, [1])])
    return inward, outward


def body(dens_blocks, basis_values, kernel, perturbation, quad_weight, point_count, active_blocks, block_pattern):
    n_mat, n_pts = lax.axis_size("mat"), lax.axis_size("pts")
    act, nact = block_pattern.shape[1], active_blocks.shape[2]
    dims = (n_mat, n_pts, act, nact)
    inward, outward = plan_of(act // n_pts)
    me_mat, me_pts = lax.axis_index("mat"), lax.axis_index("pts")

    def to_peer(value, o):
        return lax.ppermute(value, "pts", [(i, i ^ o) for i in range(n_pts)])

    points = basis_values.shape[1]
    basis = basis_values[0]
    own_active = active_blocks[0, 0]

    def across(single, values):
        if single:
            return lax.all_to_all(values, "mat", 0, 0, tiled=True)
        return [
            lax.ppermute(value, "mat", [(i, i ^ d) for i in range(n_mat)]) if d else value
            for d, value in enumerate(values)
        ]

    arrived = {}
    for single, strips in inward:
        start, rows = strips[0][0], sum(rows for at, rows in strips)
        cut = dens_blocks[:, start : start + rows]
        if not single:
            cut = [
                lax.dynamic_slice(dens_blocks, (me_mat ^ d, start, 0), (1, rows, dens_blocks.shape[2]))[0]
                for d in range(n_mat)
            ]
        arrived[start] = across(single, cut)

    peers = [own_active] + [to_peer(own_active, o) for o in range(1, n_pts)]
    pattern = lax.dynamic_index_in_dim(block_pattern, me_mat, 0, keepdims=False).reshape(-1)
    head = jnp.stack([me_mat, me_pts, point_count[0, 0]]).astype(jnp.int32)
    meta = jnp.concatenate([head] + peers + [pattern])

    flipped = transposed(basis)

    parts = {}
    for single, strips in inward:
        first = strips[0][0]
        for start, rows in strips:
            packed = pack(dims, start, rows, meta, arrived[first], start - first)
            parts[start] = [packed[0]] + [to_peer(packed[o], o) for o in range(1, n_pts)]

    raw = jnp.zeros((1, points), jnp.float32)
    for single, strips in inward:
        for start, rows in strips:
            raw = density(dims, start, rows, meta, parts[start], flipped, raw)

    inside = jnp.arange(points, dtype=jnp.int32)[None, :] < point_count[0, 0]
    n_response = jnp.where(inside, raw, 0.0)

    given = {}
    for single, strips in outward:
        for start, rows in strips:
            sent = response(dims, start, rows, meta, flipped, basis, raw, kernel, perturbation, quad_weight)
            given[start] = [sent[0]] + [to_peer(sent[o], o) for o in range(1, n_pts)]

    held = None
    for single, strips in outward:
        start, rows = strips[0][0], sum(rows for at, rows in strips)
        cut = combine(dims, strips, single, meta, sum([given[at] for at, rows in strips], []))
        back = across(single, cut[0] if single else cut)
        held = widen(dims, start, rows, dens_blocks.shape[1], meta, back, held)
    return held, n_response


def solution(mesh):
    placed = (
        P(None, "pts", "mat"),
        P("mat", "pts", None),
        P("mat", "pts"),
        P("mat", "pts"),
        P("mat", "pts"),
        P("mat", "pts"),
        P("mat", "pts", None),
        P(),
    )

    return jax.shard_map(
        body,
        mesh=mesh,
        in_specs=placed,
        out_specs=(P(None, "pts", "mat"), P("mat", "pts")),
        check_vma=False,
    )
```

```python
import functools

import jax
import jax.numpy as jnp
from jax import lax
from jax.experimental import pallas as pl
from jax.experimental.pallas import tpu as pltpu
from jax.sharding import PartitionSpec as P


BLOCK = 128
VM = pl.BlockSpec(memory_space=pltpu.VMEM)
ANY = pl.BlockSpec(memory_space=pl.ANY)
HEAD = 3
GRANT = pltpu.CompilerParams(vmem_limit_bytes=20 << 20)


def cost(flops, moved):
    return pl.CostEstimate(flops=int(flops), bytes_accessed=int(moved), transcendentals=0)


def lanes(block):
    return pl.ds(pl.multiple_of(block * BLOCK, BLOCK), BLOCK)


def pack_kernel(dims, start, meta, *refs):
    n_mat, n_pts, act, nact = dims
    arrived, packed, stage = refs[:n_mat], refs[n_mat:-1], refs[-1]
    width = arrived[0].shape[1]
    for d in range(n_mat):
        stage[:, pl.ds(pl.multiple_of((meta[0] ^ d) * width, BLOCK), width)] = arrived[d][...]
    row_block = meta[1] * (act // n_pts) + start // BLOCK
    pattern_at = HEAD + n_pts * nact + row_block * act
    for o in range(n_pts):
        for j in range(nact):
            b = meta[HEAD + o * nact + j]
            keep = meta[pattern_at + b] != 0
            value = stage[:, lanes(b)]
            packed[o][:, j * BLOCK : (j + 1) * BLOCK] = jnp.where(keep, value, jnp.zeros_like(value))


def pack(dims, start, rows, meta, arrived, skip):
    n_mat, n_pts, act, nact = dims
    width = act // n_mat * BLOCK
    return pl.pallas_call(
        functools.partial(pack_kernel, dims, start),
        out_shape=[jax.ShapeDtypeStruct((rows, nact * BLOCK), jnp.bfloat16)] * n_pts,
        grid_spec=pltpu.PrefetchScalarGridSpec(
            num_scalar_prefetch=1,
            grid=(1,),
            in_specs=[pl.BlockSpec((rows, width), lambda i, meta: (skip // rows, 0))] * n_mat,
            out_specs=[pl.BlockSpec((rows, nact * BLOCK), lambda i, meta: (0, 0))] * n_pts,
            scratch_shapes=[pltpu.VMEM((rows, act * BLOCK), jnp.bfloat16)],
        ),
        compiler_params=GRANT,
        cost_estimate=cost(0, 2 * rows * BLOCK * (act + n_pts * nact)),
    )(meta, *arrived)


def transpose_kernel(given, out):
    out[...] = given[...].T


def transposed(basis):
    points, orbitals = basis.shape
    tile = 256
    return pl.pallas_call(
        transpose_kernel,
        out_shape=jax.ShapeDtypeStruct((orbitals, points), basis.dtype),
        grid=(points // tile,),
        in_specs=[pl.BlockSpec((tile, orbitals), lambda i: (i, 0))],
        out_specs=pl.BlockSpec((orbitals, tile), lambda i: (0, i)),
        compiler_params=GRANT,
        cost_estimate=cost(0, 4 * points * orbitals),
        name="flip",
    )(basis)


def invert(dims, meta, place):
    _, _, act, nact = dims
    for a in range(act):
        place[a] = -1
    for i in range(nact):
        place[meta[HEAD + i]] = i


def rows_of(place, block, start, rows):
    spot = place[block]
    at = jnp.maximum(spot, 0) * BLOCK + start % BLOCK
    return pl.ds(pl.multiple_of(at, rows), rows), spot >= 0


def density_kernel(dims, start, rows, tile, last, meta, *refs):
    _, n_pts, act, _ = dims
    parts, flipped, before, after, place = refs[:n_pts], refs[n_pts], refs[n_pts + 1], refs[n_pts + 2], refs[n_pts + 3]
    invert(dims, meta, place)
    left = jnp.concatenate([part[...] for part in parts], axis=0)
    points = flipped.shape[1]

    @pl.loop(0, points // tile)
    def _(t):
        at = pl.ds(pl.multiple_of(t * tile, tile), tile)
        inner = jnp.dot(left, flipped[:, at], preferred_element_type=jnp.float32)
        total = before[:, at]
        for o in range(n_pts):
            where, active = rows_of(place, (meta[1] ^ o) * (act // n_pts) + start // BLOCK, start, rows)
            own = flipped[where, at].astype(jnp.float32)
            share = jnp.sum(inner[o * rows : (o + 1) * rows] * own, axis=0, keepdims=True)
            total = total + jnp.where(active, share, jnp.zeros_like(share))
        if last:
            point = t * tile + lax.broadcasted_iota(jnp.int32, total.shape, 1)
            total = jnp.where(point < meta[2], total, jnp.zeros_like(total))
        after[:, at] = total


def density(dims, start, rows, last, meta, parts, flipped, before):
    _, n_pts, act, _ = dims
    orbitals, points = flipped.shape
    return pl.pallas_call(
        functools.partial(density_kernel, dims, start, rows, 256, last),
        out_shape=jax.ShapeDtypeStruct((1, points), jnp.float32),
        in_specs=[pl.BlockSpec(memory_space=pltpu.SMEM)] + [VM] * (n_pts + 2),
        out_specs=VM,
        scratch_shapes=[pltpu.SMEM((act,), jnp.int32)],
        compiler_params=GRANT,
        cost_estimate=cost(2 * n_pts * rows * orbitals * points, 2 * orbitals * points),
    )(meta, *parts, flipped, before)


def response_kernel(dims, start, rows, tile, meta, *refs):
    _, n_pts, act, _ = dims
    flipped, basis, n, kern, pert, weight = refs[:6]
    out, place, left = refs[6 : 6 + n_pts], refs[-2], refs[-1]
    invert(dims, meta, place)
    points = flipped.shape[1]
    inside = lax.broadcasted_iota(jnp.int32, (1, points), 1) < meta[2]
    scaling = jnp.where(inside, weight[...] * (pert[...] - kern[...] * n[...]), 0.0)
    for o in range(n_pts):
        where, active = rows_of(place, (meta[1] ^ o) * (act // n_pts) + start // BLOCK, start, rows)
        own = flipped[where, :].astype(jnp.float32)
        left[o * rows : (o + 1) * rows, :] = jnp.where(active, own * scaling, 0.0).astype(jnp.bfloat16)

    @pl.loop(0, basis.shape[1] // tile)
    def _(t):
        at = pl.ds(pl.multiple_of(t * tile, tile), tile)
        block = jnp.dot(left[...], basis[:, at], preferred_element_type=jnp.float32)
        for o in range(n_pts):
            out[o][:, at] = block[o * rows : (o + 1) * rows].astype(jnp.bfloat16)


def response(dims, start, rows, meta, flipped, basis, n, kern, pert, weight):
    _, n_pts, act, _ = dims
    orbitals, points = flipped.shape
    return pl.pallas_call(
        functools.partial(response_kernel, dims, start, rows, 256),
        out_shape=[jax.ShapeDtypeStruct((rows, orbitals), jnp.bfloat16)] * n_pts,
        in_specs=[pl.BlockSpec(memory_space=pltpu.SMEM)] + [VM] * 6,
        out_specs=[VM] * n_pts,
        scratch_shapes=[
            pltpu.SMEM((act,), jnp.int32),
            pltpu.VMEM((n_pts * rows, points), jnp.bfloat16),
        ],
        compiler_params=GRANT,
        cost_estimate=cost(2 * n_pts * rows * orbitals * points, 4 * orbitals * points),
    )(meta, flipped, basis, n, kern, pert, weight)


def combine_kernel(dims, strips, meta, *refs):
    n_mat, n_pts, act, nact = dims
    given = len(strips) * n_pts
    out, total = refs[given:-1], refs[-1]
    each = act // n_mat
    done = 0
    for s, (start, rows) in enumerate(strips):
        total[...] = jnp.zeros_like(total)
        for o in range(n_pts):
            part = refs[s * n_pts + o]
            for j in range(nact):
                b = meta[HEAD + o * nact + j]
                total[:rows, lanes(b)] += part[:, j * BLOCK : (j + 1) * BLOCK].astype(jnp.float32)
        row_block = meta[1] * (act // n_pts) + start // BLOCK
        pattern_at = HEAD + n_pts * nact + row_block * act
        for d in range(n_mat):
            for k in range(each):
                b = (meta[0] ^ d) * each + k
                keep = meta[pattern_at + b] != 0
                value = total[:rows, lanes(b)]
                value = jnp.where(keep, value, jnp.zeros_like(value)).astype(jnp.bfloat16)
                out[d][done : done + rows, k * BLOCK : (k + 1) * BLOCK] = value
        done += rows


def combine(dims, strips, meta, given):
    n_mat, n_pts, act, nact = dims
    rows = sum(rows for start, rows in strips)
    return pl.pallas_call(
        functools.partial(combine_kernel, dims, strips),
        out_shape=[jax.ShapeDtypeStruct((rows, act // n_mat * BLOCK), jnp.bfloat16)] * n_mat,
        in_specs=[pl.BlockSpec(memory_space=pltpu.SMEM)] + [VM] * len(given),
        out_specs=[VM] * n_mat,
        scratch_shapes=[pltpu.VMEM((BLOCK, act * BLOCK), jnp.float32)],
        compiler_params=GRANT,
        cost_estimate=cost(0, 2 * rows * BLOCK * (act + n_pts * nact)),
    )(meta, *given)


def widen_kernel(n_mat, meta, *refs):
    out = refs[-1]
    for d in range(n_mat):
        out[meta[0] ^ d] = refs[d][...].astype(jnp.float32)


def widen(dims, start, rows, all_rows, meta, given, held):
    n_mat, _, act, _ = dims
    width = act // n_mat * BLOCK
    more = [] if held is None else [held]
    return pl.pallas_call(
        functools.partial(widen_kernel, n_mat),
        out_shape=jax.ShapeDtypeStruct((n_mat, all_rows, width), jnp.float32),
        grid_spec=pltpu.PrefetchScalarGridSpec(
            num_scalar_prefetch=1,
            grid=(1,),
            in_specs=[pl.BlockSpec((rows, width), lambda i, meta: (0, 0))] * n_mat + [ANY] * len(more),
            out_specs=pl.BlockSpec((n_mat, rows, width), lambda i, meta: (0, start // rows, 0)),
        ),
        input_output_aliases={} if held is None else {1 + n_mat: 0},
        compiler_params=GRANT,
        cost_estimate=cost(0, 6 * rows * n_mat * width),
    )(meta, *given, *more)


def chunks(row_blocks, shape):
    half = BLOCK // 2
    if sum(sum(sizes) for sizes in shape) != 2 * row_blocks:
        shape = [[2]] * row_blocks
    out, at = [], 0
    for sizes in shape:
        strips = []
        for size in sizes:
            strips.append((at, size * half))
            at += size * half
        out.append(tuple(strips))
    return out


def plan_of(row_blocks):
    inward = chunks(row_blocks, [[2], [2], [2, 1, 1]])
    outward = chunks(row_blocks, [[1, 1], [2], [2], [1, 1]])
    return inward, outward


def body(dens_blocks, basis_values, kernel, perturbation, quad_weight, point_count, active_blocks, block_pattern):
    n_mat, n_pts = lax.axis_size("mat"), lax.axis_size("pts")
    act, nact = block_pattern.shape[1], active_blocks.shape[2]
    dims = (n_mat, n_pts, act, nact)
    inward, outward = plan_of(act // n_pts)
    me_mat, me_pts = lax.axis_index("mat"), lax.axis_index("pts")

    def to_peer(value, o):
        return lax.ppermute(value, "pts", [(i, i ^ o) for i in range(n_pts)])

    points = basis_values.shape[1]
    basis = basis_values[0]
    own_active = active_blocks[0, 0]

    def across(values):
        out = [values[0]]
        for d in range(1, n_mat):
            out.append(lax.ppermute(values[d], "mat", [(i, i ^ d) for i in range(n_mat)]))
        return out

    arrived = {}
    for strips in inward:
        start, rows = strips[0][0], sum(rows for at, rows in strips)
        cut = [
            lax.dynamic_slice(dens_blocks, (me_mat ^ d, start, 0), (1, rows, dens_blocks.shape[2]))[0]
            for d in range(n_mat)
        ]
        arrived[start] = across(cut)

    peers = [own_active] + [to_peer(own_active, o) for o in range(1, n_pts)]
    pattern = lax.dynamic_index_in_dim(block_pattern, me_mat, 0, keepdims=False).reshape(-1)
    head = jnp.stack([me_mat, me_pts, point_count[0, 0]]).astype(jnp.int32)
    meta = jnp.concatenate([head] + peers + [pattern])

    flipped = transposed(basis)

    parts = {}
    for strips in inward:
        first = strips[0][0]
        for start, rows in strips:
            packed = pack(dims, start, rows, meta, arrived[first], start - first)
            parts[start] = [packed[0]] + [to_peer(packed[o], o) for o in range(1, n_pts)]

    n = jnp.zeros((1, points), jnp.float32)
    for strips in inward:
        for start, rows in strips:
            last = start + rows == dens_blocks.shape[1]
            n = density(dims, start, rows, last, meta, parts[start], flipped, n)

    given = {}
    for strips in outward:
        for start, rows in strips:
            sent = response(dims, start, rows, meta, flipped, basis, n, kernel, perturbation, quad_weight)
            given[start] = [sent[0]] + [to_peer(sent[o], o) for o in range(1, n_pts)]

    held = None
    for strips in outward:
        start, rows = strips[0][0], sum(rows for at, rows in strips)
        cut = combine(dims, strips, meta, sum([given[at] for at, rows in strips], []))
        back = across(cut)
        held = widen(dims, start, rows, dens_blocks.shape[1], meta, back, held)
    return held, n


def solution(mesh):
    placed = (
        P(None, "pts", "mat"),
        P("mat", "pts", None),
        P("mat", "pts"),
        P("mat", "pts"),
        P("mat", "pts"),
        P("mat", "pts"),
        P("mat", "pts", None),
        P(),
    )

    return jax.shard_map(
        body,
        mesh=mesh,
        in_specs=placed,
        out_specs=(P(None, "pts", "mat"), P("mat", "pts")),
        check_vma=False,
    )
```

```python
import functools

import jax
import jax.numpy as jnp
from jax import lax
from jax.experimental import pallas as pl
from jax.experimental.pallas import tpu as pltpu
from jax.sharding import PartitionSpec as P


BLOCK = 128
VM = pl.BlockSpec(memory_space=pltpu.VMEM)
ANY = pl.BlockSpec(memory_space=pl.ANY)
HEAD = 3
GRANT = pltpu.CompilerParams(vmem_limit_bytes=20 << 20)


def cost(flops, moved):
    return pl.CostEstimate(flops=int(flops), bytes_accessed=int(moved), transcendentals=0)


def lanes(block):
    return pl.ds(pl.multiple_of(block * BLOCK, BLOCK), BLOCK)


def pack_kernel(dims, start, meta, *refs):
    n_mat, n_pts, act, nact = dims
    arrived, packed, stage = refs[:n_mat], refs[n_mat:-1], refs[-1]
    width = arrived[0].shape[1]
    for d in range(n_mat):
        stage[:, pl.ds(pl.multiple_of((meta[0] ^ d) * width, BLOCK), width)] = arrived[d][...]
    row_block = meta[1] * (act // n_pts) + start // BLOCK
    pattern_at = HEAD + n_pts * nact + row_block * act
    for o in range(n_pts):
        for j in range(nact):
            b = meta[HEAD + o * nact + j]
            keep = meta[pattern_at + b] != 0
            value = stage[:, lanes(b)]
            packed[o][:, j * BLOCK : (j + 1) * BLOCK] = jnp.where(keep, value, jnp.zeros_like(value))


def pack(dims, start, rows, meta, arrived, skip):
    n_mat, n_pts, act, nact = dims
    width = act // n_mat * BLOCK
    return pl.pallas_call(
        functools.partial(pack_kernel, dims, start),
        out_shape=[jax.ShapeDtypeStruct((rows, nact * BLOCK), jnp.bfloat16)] * n_pts,
        grid_spec=pltpu.PrefetchScalarGridSpec(
            num_scalar_prefetch=1,
            grid=(1,),
            in_specs=[pl.BlockSpec((rows, width), lambda i, meta: (skip // rows, 0))] * n_mat,
            out_specs=[pl.BlockSpec((rows, nact * BLOCK), lambda i, meta: (0, 0))] * n_pts,
            scratch_shapes=[pltpu.VMEM((rows, act * BLOCK), jnp.bfloat16)],
        ),
        compiler_params=GRANT,
        cost_estimate=cost(0, 2 * rows * BLOCK * (act + n_pts * nact)),
    )(meta, *arrived)


def transpose_kernel(given, out):
    out[...] = given[...].T


def transposed(basis):
    points, orbitals = basis.shape
    tile = 256
    return pl.pallas_call(
        transpose_kernel,
        out_shape=jax.ShapeDtypeStruct((orbitals, points), basis.dtype),
        grid=(points // tile,),
        in_specs=[pl.BlockSpec((tile, orbitals), lambda i: (i, 0))],
        out_specs=pl.BlockSpec((orbitals, tile), lambda i: (0, i)),
        compiler_params=GRANT,
        cost_estimate=cost(0, 4 * points * orbitals),
        name="flip",
    )(basis)


def invert(dims, meta, place):
    _, _, act, nact = dims
    for a in range(act):
        place[a] = -1
    for i in range(nact):
        place[meta[HEAD + i]] = i


def rows_of(place, block, start, rows):
    spot = place[block]
    at = jnp.maximum(spot, 0) * BLOCK + start % BLOCK
    return pl.ds(pl.multiple_of(at, rows), rows), spot >= 0


def density_kernel(dims, start, rows, tile, last, meta, *refs):
    _, n_pts, act, _ = dims
    parts, flipped, before, after, place = refs[:n_pts], refs[n_pts], refs[n_pts + 1], refs[n_pts + 2], refs[n_pts + 3]
    invert(dims, meta, place)
    left = jnp.concatenate([part[...] for part in parts], axis=0)
    points = flipped.shape[1]

    @pl.loop(0, points // tile)
    def _(t):
        at = pl.ds(pl.multiple_of(t * tile, tile), tile)
        inner = jnp.dot(left, flipped[:, at], preferred_element_type=jnp.float32)
        total = before[:, at]
        for o in range(n_pts):
            where, active = rows_of(place, (meta[1] ^ o) * (act // n_pts) + start // BLOCK, start, rows)
            own = flipped[where, at].astype(jnp.float32)
            share = jnp.sum(inner[o * rows : (o + 1) * rows] * own, axis=0, keepdims=True)
            total = total + jnp.where(active, share, jnp.zeros_like(share))
        if last:
            point = t * tile + lax.broadcasted_iota(jnp.int32, total.shape, 1)
            total = jnp.where(point < meta[2], total, jnp.zeros_like(total))
        after[:, at] = total


def density(dims, start, rows, last, meta, parts, flipped, before):
    _, n_pts, act, _ = dims
    orbitals, points = flipped.shape
    return pl.pallas_call(
        functools.partial(density_kernel, dims, start, rows, 256, last),
        out_shape=jax.ShapeDtypeStruct((1, points), jnp.float32),
        in_specs=[pl.BlockSpec(memory_space=pltpu.SMEM)] + [VM] * (n_pts + 2),
        out_specs=VM,
        scratch_shapes=[pltpu.SMEM((act,), jnp.int32)],
        compiler_params=GRANT,
        cost_estimate=cost(2 * n_pts * rows * orbitals * points, 2 * orbitals * points),
    )(meta, *parts, flipped, before)


def response_kernel(dims, start, rows, tile, meta, *refs):
    _, n_pts, act, _ = dims
    flipped, basis, n, kern, pert, weight = refs[:6]
    out, place, left = refs[6 : 6 + n_pts], refs[-2], refs[-1]
    invert(dims, meta, place)
    points = flipped.shape[1]
    inside = lax.broadcasted_iota(jnp.int32, (1, points), 1) < meta[2]
    scaling = jnp.where(inside, weight[...] * (pert[...] - kern[...] * n[...]), 0.0)
    for o in range(n_pts):
        where, active = rows_of(place, (meta[1] ^ o) * (act // n_pts) + start // BLOCK, start, rows)
        own = flipped[where, :].astype(jnp.float32)
        left[o * rows : (o + 1) * rows, :] = jnp.where(active, own * scaling, 0.0).astype(jnp.bfloat16)

    @pl.loop(0, basis.shape[1] // tile)
    def _(t):
        at = pl.ds(pl.multiple_of(t * tile, tile), tile)
        block = jnp.dot(left[...], basis[:, at], preferred_element_type=jnp.float32)
        for o in range(n_pts):
            out[o][:, at] = block[o * rows : (o + 1) * rows].astype(jnp.bfloat16)


def response(dims, start, rows, meta, flipped, basis, n, kern, pert, weight):
    _, n_pts, act, _ = dims
    orbitals, points = flipped.shape
    return pl.pallas_call(
        functools.partial(response_kernel, dims, start, rows, 256),
        out_shape=[jax.ShapeDtypeStruct((rows, orbitals), jnp.bfloat16)] * n_pts,
        in_specs=[pl.BlockSpec(memory_space=pltpu.SMEM)] + [VM] * 6,
        out_specs=[VM] * n_pts,
        scratch_shapes=[
            pltpu.SMEM((act,), jnp.int32),
            pltpu.VMEM((n_pts * rows, points), jnp.bfloat16),
        ],
        compiler_params=GRANT,
        cost_estimate=cost(2 * n_pts * rows * orbitals * points, 4 * orbitals * points),
    )(meta, flipped, basis, n, kern, pert, weight)


def combine_kernel(dims, strips, meta, *refs):
    n_mat, n_pts, act, nact = dims
    given = len(strips) * n_pts
    out, total = refs[given:-1], refs[-1]
    each = act // n_mat
    done = 0
    for s, (start, rows) in enumerate(strips):
        total[...] = jnp.zeros_like(total)
        for o in range(n_pts):
            part = refs[s * n_pts + o]
            for j in range(nact):
                b = meta[HEAD + o * nact + j]
                total[:rows, lanes(b)] += part[:, j * BLOCK : (j + 1) * BLOCK].astype(jnp.float32)
        row_block = meta[1] * (act // n_pts) + start // BLOCK
        pattern_at = HEAD + n_pts * nact + row_block * act
        for d in range(n_mat):
            for k in range(each):
                b = (meta[0] ^ d) * each + k
                keep = meta[pattern_at + b] != 0
                value = total[:rows, lanes(b)]
                value = jnp.where(keep, value, jnp.zeros_like(value)).astype(jnp.bfloat16)
                out[d][done : done + rows, k * BLOCK : (k + 1) * BLOCK] = value
        done += rows


def combine(dims, strips, meta, given):
    n_mat, n_pts, act, nact = dims
    rows = sum(rows for start, rows in strips)
    return pl.pallas_call(
        functools.partial(combine_kernel, dims, strips),
        out_shape=[jax.ShapeDtypeStruct((rows, act // n_mat * BLOCK), jnp.bfloat16)] * n_mat,
        in_specs=[pl.BlockSpec(memory_space=pltpu.SMEM)] + [VM] * len(given),
        out_specs=[VM] * n_mat,
        scratch_shapes=[pltpu.VMEM((BLOCK, act * BLOCK), jnp.float32)],
        compiler_params=GRANT,
        cost_estimate=cost(0, 2 * rows * BLOCK * (act + n_pts * nact)),
    )(meta, *given)


def widen_kernel(n_mat, meta, *refs):
    out = refs[-1]
    for d in range(n_mat):
        out[meta[0] ^ d] = refs[d][...].astype(jnp.float32)


def widen(dims, start, rows, all_rows, meta, given, held):
    n_mat, _, act, _ = dims
    width = act // n_mat * BLOCK
    more = [] if held is None else [held]
    return pl.pallas_call(
        functools.partial(widen_kernel, n_mat),
        out_shape=jax.ShapeDtypeStruct((n_mat, all_rows, width), jnp.float32),
        grid_spec=pltpu.PrefetchScalarGridSpec(
            num_scalar_prefetch=1,
            grid=(1,),
            in_specs=[pl.BlockSpec((rows, width), lambda i, meta: (0, 0))] * n_mat + [ANY] * len(more),
            out_specs=pl.BlockSpec((n_mat, rows, width), lambda i, meta: (0, start // rows, 0)),
        ),
        input_output_aliases={} if held is None else {1 + n_mat: 0},
        compiler_params=GRANT,
        cost_estimate=cost(0, 6 * rows * n_mat * width),
    )(meta, *given, *more)


def chunks(row_blocks, shape):
    half = BLOCK // 2
    if sum(sum(sizes) for sizes in shape) != 2 * row_blocks:
        shape = [[2]] * row_blocks
    out, at = [], 0
    for sizes in shape:
        strips = []
        for size in sizes:
            strips.append((at, size * half))
            at += size * half
        out.append(tuple(strips))
    return out


def plan_of(row_blocks):
    inward = chunks(row_blocks, [[2], [2], [2, 1, 1]])
    outward = chunks(row_blocks, [[2], [2], [2], [2]])
    return inward, outward


def body(dens_blocks, basis_values, kernel, perturbation, quad_weight, point_count, active_blocks, block_pattern):
    n_mat, n_pts = lax.axis_size("mat"), lax.axis_size("pts")
    act, nact = block_pattern.shape[1], active_blocks.shape[2]
    dims = (n_mat, n_pts, act, nact)
    inward, outward = plan_of(act // n_pts)
    me_mat, me_pts = lax.axis_index("mat"), lax.axis_index("pts")

    def to_peer(value, o):
        return lax.ppermute(value, "pts", [(i, i ^ o) for i in range(n_pts)])

    points = basis_values.shape[1]
    basis = basis_values[0]
    own_active = active_blocks[0, 0]

    def across(values):
        out = [values[0]] + [None] * (n_mat - 1)
        for d in range(n_mat - 1, 0, -1):
            out[d] = lax.ppermute(values[d], "mat", [(i, i ^ d) for i in range(n_mat)])
        return out

    arrived = {}
    for strips in inward:
        start, rows = strips[0][0], sum(rows for at, rows in strips)
        cut = [
            lax.dynamic_slice(dens_blocks, (me_mat ^ d, start, 0), (1, rows, dens_blocks.shape[2]))[0]
            for d in range(n_mat)
        ]
        arrived[start] = across(cut)

    peers = [own_active] + [to_peer(own_active, o) for o in range(1, n_pts)]
    pattern = lax.dynamic_index_in_dim(block_pattern, me_mat, 0, keepdims=False).reshape(-1)
    head = jnp.stack([me_mat, me_pts, point_count[0, 0]]).astype(jnp.int32)
    meta = jnp.concatenate([head] + peers + [pattern])

    flipped = transposed(basis)

    parts = {}
    for strips in inward:
        first = strips[0][0]
        for start, rows in strips:
            packed = pack(dims, start, rows, meta, arrived[first], start - first)
            parts[start] = [packed[0]] + [to_peer(packed[o], o) for o in range(1, n_pts)]

    n = jnp.zeros((1, points), jnp.float32)
    for strips in inward:
        for start, rows in strips:
            last = start + rows == dens_blocks.shape[1]
            n = density(dims, start, rows, last, meta, parts[start], flipped, n)

    given = {}
    for strips in outward:
        for start, rows in strips:
            sent = response(dims, start, rows, meta, flipped, basis, n, kernel, perturbation, quad_weight)
            given[start] = [sent[0]] + [to_peer(sent[o], o) for o in range(1, n_pts)]

    held = None
    for strips in outward:
        start, rows = strips[0][0], sum(rows for at, rows in strips)
        cut = combine(dims, strips, meta, sum([given[at] for at, rows in strips], []))
        back = across(cut)
        held = widen(dims, start, rows, dens_blocks.shape[1], meta, back, held)
    return held, n


def solution(mesh):
    placed = (
        P(None, "pts", "mat"),
        P("mat", "pts", None),
        P("mat", "pts"),
        P("mat", "pts"),
        P("mat", "pts"),
        P("mat", "pts"),
        P("mat", "pts", None),
        P(),
    )

    return jax.shard_map(
        body,
        mesh=mesh,
        in_specs=placed,
        out_specs=(P(None, "pts", "mat"), P("mat", "pts")),
        check_vma=False,
    )
```

```python
import functools

import jax
import jax.numpy as jnp
from jax import lax
from jax.experimental import pallas as pl
from jax.experimental.pallas import tpu as pltpu
from jax.sharding import PartitionSpec as P


BLOCK = 128
VM = pl.BlockSpec(memory_space=pltpu.VMEM)
ANY = pl.BlockSpec(memory_space=pl.ANY)
HEAD = 3
GRANT = pltpu.CompilerParams(vmem_limit_bytes=20 << 20)


def cost(flops, moved):
    return pl.CostEstimate(flops=int(flops), bytes_accessed=int(moved), transcendentals=0)


def lanes(block):
    return pl.ds(pl.multiple_of(block * BLOCK, BLOCK), BLOCK)


def rows_at(block):
    return pl.ds(pl.multiple_of(block * BLOCK, BLOCK), BLOCK)


def active_rows(dims, meta, o, column):
    _, n_pts, act, nact = dims
    out = []
    for r in range(act // n_pts):
        found = jnp.int32(0)
        for j in range(nact):
            found += (meta[HEAD + o * nact + j] == column * (act // n_pts) + r).astype(jnp.int32)
        out.append(found)
    return out


def ranked_row(flags, rank, from_end):
    row, passed = jnp.int32(-1), jnp.int32(0)
    order = range(len(flags) - 1, -1, -1) if from_end else range(len(flags))
    for r in order:
        row = jnp.where((flags[r] != 0) & (passed == rank), r, row)
        passed += flags[r]
    return row


def list_slots(dims, meta, table, o, column, row, lower, positions):
    _, n_pts, act, nact = dims
    each = act // n_pts
    base, filled = o * (nact + 1), jnp.int32(0)
    for j in range(nact + 1):
        table[base + j] = 0
    for j in range(nact):
        block = meta[HEAD + (0 if positions else o) * nact + j]
        local = block - column * each
        kept = (local < 0) | (local >= each) | ((local <= row) if lower else (local >= row))
        table[base + filled] = j if positions else block
        filled += kept.astype(jnp.int32)


def slots_in(dims, k):
    return dims[3] - dims[2] // dims[1] + 1 + k


def slots_out(dims, k):
    return dims[3] - k


def pack_kernel(dims, k, meta, *refs):
    n_mat, n_pts, act, nact = dims
    each = act // n_pts
    arrived, earlier = refs[:n_mat], refs[n_mat : n_mat + k]
    stage, packed, table = refs[n_mat + k], refs[n_mat + k + 1 : -1], refs[-1]
    width = arrived[0].shape[1]
    me_pts = meta[1]
    pattern_at = HEAD + n_pts * nact + (me_pts * each + k) * act
    for d in range(n_mat):
        m = meta[0] ^ d
        for c in range(width // BLOCK):
            b = m * (width // BLOCK) + c
            value = arrived[d][:, c * BLOCK : (c + 1) * BLOCK]
            stage[:, lanes(b)] = jnp.where(meta[pattern_at + b] != 0, value, jnp.zeros_like(value))
    for r in range(k):
        mine, other = me_pts * each + r, me_pts * each + k
        pair = stage[:, lanes(mine)].astype(jnp.float32) + earlier[r][:, lanes(other)].astype(jnp.float32).T
        stage[:, lanes(mine)] = pair.astype(jnp.bfloat16)
    for o in range(n_pts):
        flags = active_rows(dims, meta, o, me_pts)
        row = jnp.maximum(ranked_row(flags, each - 1 - k, True), 0)
        list_slots(dims, meta, table, o, me_pts, row, True, False)
        for r in range(k + 1):
            source = stage if r == k else earlier[r]

            @pl.when(row == r)
            def _(source=source, o=o):
                for slot in range(slots_in(dims, k)):
                    b = table[o * (nact + 1) + slot]
                    packed[o][:, slot * BLOCK : (slot + 1) * BLOCK] = source[:, lanes(b)]


def pack(dims, k, meta, arrived, earlier):
    n_mat, n_pts, act, nact = dims
    shapes = [jax.ShapeDtypeStruct((BLOCK, act * BLOCK), jnp.bfloat16)]
    shapes += [jax.ShapeDtypeStruct((BLOCK, slots_in(dims, k) * BLOCK), jnp.bfloat16)] * n_pts
    out = pl.pallas_call(
        functools.partial(pack_kernel, dims, k),
        out_shape=shapes,
        in_specs=[pl.BlockSpec(memory_space=pltpu.SMEM)] + [VM] * (n_mat + k),
        out_specs=[VM] * len(shapes),
        scratch_shapes=[pltpu.SMEM((n_pts * (nact + 1),), jnp.int32)],
        compiler_params=GRANT,
        cost_estimate=cost(0, 2 * BLOCK * BLOCK * (act + n_pts * nact)),
    )(meta, *arrived, *earlier)
    return out[0], out[1:]


def transpose_kernel(given, out):
    out[...] = given[...].T


def transposed(basis):
    points, orbitals = basis.shape
    tile = 256
    return pl.pallas_call(
        transpose_kernel,
        out_shape=jax.ShapeDtypeStruct((orbitals, points), basis.dtype),
        grid=(points // tile,),
        in_specs=[pl.BlockSpec((tile, orbitals), lambda i: (i, 0))],
        out_specs=pl.BlockSpec((orbitals, tile), lambda i: (0, i)),
        compiler_params=GRANT,
        cost_estimate=cost(0, 4 * points * orbitals),
        name="flip",
    )(basis)


def invert(dims, meta, place):
    _, _, act, nact = dims
    for a in range(act):
        place[a] = -1
    for i in range(nact):
        place[meta[HEAD + i]] = i


def density_kernel(dims, k, tile, last, meta, *refs):
    _, n_pts, act, nact = dims
    each = act // n_pts
    parts, flipped, before, after, place, table, left = refs[:n_pts], *refs[n_pts:]
    invert(dims, meta, place)
    points = flipped.shape[1]
    rows = []
    left[...] = jnp.zeros_like(left)
    for o in range(n_pts):
        column = meta[1] ^ o
        row = ranked_row(active_rows(dims, meta, 0, column), each - 1 - k, True)
        list_slots(dims, meta, table, o, column, jnp.maximum(row, 0), True, True)
        rows.append((jnp.maximum(place[column * each + jnp.maximum(row, 0)], 0), row >= 0))
        for slot in range(slots_in(dims, k)):
            j = table[o * (nact + 1) + slot]
            left[o * BLOCK : (o + 1) * BLOCK, lanes(j)] = parts[o][:, slot * BLOCK : (slot + 1) * BLOCK]

    @pl.loop(0, points // tile)
    def _(t):
        at = pl.ds(pl.multiple_of(t * tile, tile), tile)
        inner = jnp.dot(left[...], flipped[:, at], preferred_element_type=jnp.float32)
        total = before[:, at]
        for o, (spot, valid) in enumerate(rows):
            own = flipped[rows_at(spot), at].astype(jnp.float32)
            share = jnp.sum(inner[o * BLOCK : (o + 1) * BLOCK] * own, axis=0, keepdims=True)
            total = total + jnp.where(valid, share, jnp.zeros_like(share))
        if last:
            point = t * tile + lax.broadcasted_iota(jnp.int32, total.shape, 1)
            total = jnp.where(point < meta[2], total, jnp.zeros_like(total))
        after[:, at] = total


def density(dims, k, last, meta, parts, flipped, before):
    _, n_pts, act, nact = dims
    orbitals, points = flipped.shape
    return pl.pallas_call(
        functools.partial(density_kernel, dims, k, 256, last),
        out_shape=jax.ShapeDtypeStruct((1, points), jnp.float32),
        in_specs=[pl.BlockSpec(memory_space=pltpu.SMEM)] + [VM] * (n_pts + 2),
        out_specs=VM,
        scratch_shapes=[
            pltpu.SMEM((act,), jnp.int32),
            pltpu.SMEM((n_pts * (nact + 1),), jnp.int32),
            pltpu.VMEM((n_pts * BLOCK, orbitals), jnp.bfloat16),
        ],
        compiler_params=GRANT,
        cost_estimate=cost(2 * n_pts * BLOCK * orbitals * points, 2 * orbitals * points),
    )(meta, *parts, flipped, before)


def response_kernel(dims, k, tile, meta, *refs):
    _, n_pts, act, nact = dims
    each = act // n_pts
    flipped, basis, n, kern, pert, weight = refs[:6]
    out, (place, table, left, right) = refs[6 : 6 + n_pts], refs[6 + n_pts :]
    invert(dims, meta, place)
    points = flipped.shape[1]
    inside = lax.broadcasted_iota(jnp.int32, (1, points), 1) < meta[2]
    scaling = jnp.where(inside, weight[...] * (pert[...] - kern[...] * n[...]), 0.0)
    for o in range(n_pts):
        column = meta[1] ^ o
        row = ranked_row(active_rows(dims, meta, 0, column), k, False)
        list_slots(dims, meta, table, o, column, jnp.maximum(row, 0), False, True)
        spot = jnp.maximum(place[column * each + jnp.maximum(row, 0)], 0)
        own = flipped[rows_at(spot), :].astype(jnp.float32)
        left[o * BLOCK : (o + 1) * BLOCK, :] = jnp.where(row >= 0, own * scaling, 0.0).astype(jnp.bfloat16)

    @pl.loop(0, basis.shape[1] // tile)
    def _(t):
        at = pl.ds(pl.multiple_of(t * tile, tile), tile)
        right[:, at] = jnp.dot(left[...], basis[:, at], preferred_element_type=jnp.float32).astype(jnp.bfloat16)

    for o in range(n_pts):
        for slot in range(slots_out(dims, k)):
            j = table[o * (nact + 1) + slot]
            out[o][:, slot * BLOCK : (slot + 1) * BLOCK] = right[o * BLOCK : (o + 1) * BLOCK, lanes(j)]


def response(dims, k, meta, flipped, basis, n, kern, pert, weight):
    _, n_pts, act, nact = dims
    orbitals, points = flipped.shape
    return pl.pallas_call(
        functools.partial(response_kernel, dims, k, 256),
        out_shape=[jax.ShapeDtypeStruct((BLOCK, slots_out(dims, k) * BLOCK), jnp.bfloat16)] * n_pts,
        in_specs=[pl.BlockSpec(memory_space=pltpu.SMEM)] + [VM] * 6,
        out_specs=[VM] * n_pts,
        scratch_shapes=[
            pltpu.SMEM((act,), jnp.int32),
            pltpu.SMEM((n_pts * (nact + 1),), jnp.int32),
            pltpu.VMEM((n_pts * BLOCK, points), jnp.bfloat16),
            pltpu.VMEM((n_pts * BLOCK, orbitals), jnp.bfloat16),
        ],
        compiler_params=GRANT,
        cost_estimate=cost(2 * n_pts * BLOCK * orbitals * points, 4 * orbitals * points),
    )(meta, flipped, basis, n, kern, pert, weight)


def combine_kernel(dims, k, meta, *refs):
    n_mat, n_pts, act, nact = dims
    each = act // n_pts
    strips, before = refs[: (k + 1) * n_pts], refs[(k + 1) * n_pts : (k + 1) * n_pts + k]
    out, (inner, total, table, held, sem) = refs[(k + 1) * n_pts + k : -5], refs[-5:]
    me_pts = meta[1]
    first = me_pts * each
    ranks = []
    for o in range(n_pts):
        flags = active_rows(dims, meta, o, me_pts)
        ranks.append(jnp.where(flags[k] != 0, sum(flags[:k], jnp.int32(0)), -1))
        for i in range(k + 1):

            @pl.when(ranks[o] == i)
            def _(o=o, i=i):
                filled = slots_out(dims, i) * BLOCK
                pltpu.make_async_copy(strips[i * n_pts + o], held.at[o, :, :filled], sem.at[o]).start()

        list_slots(dims, meta, table, o, me_pts, jnp.int32(k), False, False)
    total[...] = jnp.zeros_like(total)
    for o in range(n_pts):
        for i in range(k + 1):

            @pl.when(ranks[o] == i)
            def _(o=o, i=i):
                filled = slots_out(dims, i) * BLOCK
                pltpu.make_async_copy(strips[i * n_pts + o], held.at[o, :, :filled], sem.at[o]).wait()
                for slot in range(slots_out(dims, i)):
                    b = table[o * (nact + 1) + slot]
                    part = held[o, :, slot * BLOCK : (slot + 1) * BLOCK].astype(jnp.float32)
                    total[:, lanes(b)] += part

    for r in range(k):
        total[:, lanes(first + r)] = before[r][:, k * BLOCK : (k + 1) * BLOCK].T
    for r in range(each):
        inner[:, r * BLOCK : (r + 1) * BLOCK] = total[:, lanes(first + r)]
    width = act // n_mat
    pattern_at = HEAD + n_pts * nact + (first + k) * act
    for d in range(n_mat):
        for c in range(width):
            b = (meta[0] ^ d) * width + c
            value = total[:, lanes(b)]
            value = jnp.where(meta[pattern_at + b] != 0, value, jnp.zeros_like(value))
            out[d][:, c * BLOCK : (c + 1) * BLOCK] = value.astype(jnp.bfloat16)


def combine(dims, k, meta, strips, before):
    n_mat, n_pts, act, nact = dims
    shapes = [jax.ShapeDtypeStruct((BLOCK, act // n_mat * BLOCK), jnp.bfloat16)] * n_mat
    shapes += [jax.ShapeDtypeStruct((BLOCK, act // n_pts * BLOCK), jnp.float32)]
    given = sum(strips, [])
    out = pl.pallas_call(
        functools.partial(combine_kernel, dims, k),
        out_shape=shapes,
        in_specs=[pl.BlockSpec(memory_space=pltpu.SMEM)] + [ANY] * len(given) + [VM] * k,
        out_specs=[VM] * len(shapes),
        scratch_shapes=[
            pltpu.VMEM((BLOCK, act * BLOCK), jnp.float32),
            pltpu.SMEM((n_pts * (nact + 1),), jnp.int32),
            pltpu.VMEM((n_pts, BLOCK, nact * BLOCK), jnp.bfloat16),
            pltpu.SemaphoreType.DMA((n_pts,)),
        ],
        compiler_params=GRANT,
        cost_estimate=cost(0, 2 * BLOCK * BLOCK * (act + n_pts * nact)),
    )(meta, *given, *before)
    return out[:-1], out[-1]


def widen_kernel(n_mat, meta, *refs):
    out = refs[-1]
    for d in range(n_mat):
        out[meta[0] ^ d] = refs[d][...].astype(jnp.float32)


def widen(dims, start, rows, all_rows, meta, given, held):
    n_mat, _, act, _ = dims
    width = act // n_mat * BLOCK
    more = [] if held is None else [held]
    return pl.pallas_call(
        functools.partial(widen_kernel, n_mat),
        out_shape=jax.ShapeDtypeStruct((n_mat, all_rows, width), jnp.float32),
        grid_spec=pltpu.PrefetchScalarGridSpec(
            num_scalar_prefetch=1,
            grid=(1,),
            in_specs=[pl.BlockSpec((rows, width), lambda i, meta: (0, 0))] * n_mat + [ANY] * len(more),
            out_specs=pl.BlockSpec((n_mat, rows, width), lambda i, meta: (0, start // rows, 0)),
        ),
        input_output_aliases={} if held is None else {1 + n_mat: 0},
        compiler_params=GRANT,
        cost_estimate=cost(0, 6 * rows * n_mat * width),
    )(meta, *given, *more)


def body(dens_blocks, basis_values, kernel, perturbation, quad_weight, point_count, active_blocks, block_pattern):
    n_mat, n_pts = lax.axis_size("mat"), lax.axis_size("pts")
    act, nact = block_pattern.shape[1], active_blocks.shape[2]
    dims = (n_mat, n_pts, act, nact)
    row_blocks = act // n_pts
    me_mat, me_pts = lax.axis_index("mat"), lax.axis_index("pts")

    def to_peer(value, o):
        return lax.ppermute(value, "pts", [(i, i ^ o) for i in range(n_pts)])

    points = basis_values.shape[1]
    basis = basis_values[0]
    own_active = active_blocks[0, 0]

    def across(values):
        out = [values[0]] + [None] * (n_mat - 1)
        for d in range(n_mat - 1, 0, -1):
            out[d] = lax.ppermute(values[d], "mat", [(i, i ^ d) for i in range(n_mat)])
        return out

    arrived = []
    for k in range(row_blocks):
        cut = [
            lax.dynamic_slice(dens_blocks, (me_mat ^ d, k * BLOCK, 0), (1, BLOCK, dens_blocks.shape[2]))[0]
            for d in range(n_mat)
        ]
        arrived.append(across(cut))

    peers = [own_active] + [to_peer(own_active, o) for o in range(1, n_pts)]
    pattern = lax.dynamic_index_in_dim(block_pattern, me_mat, 0, keepdims=False).reshape(-1)
    head = jnp.stack([me_mat, me_pts, point_count[0, 0]]).astype(jnp.int32)
    meta = jnp.concatenate([head] + peers + [pattern])

    flipped = transposed(basis)

    parts, stages = [], []
    for k in range(row_blocks):
        held, packed = pack(dims, k, meta, arrived[k], stages)
        stages.append(held)
        parts.append([packed[0]] + [to_peer(packed[o], o) for o in range(1, n_pts)])

    n = jnp.zeros((1, points), jnp.float32)
    for k in range(row_blocks):
        n = density(dims, k, k == row_blocks - 1, meta, parts[k], flipped, n)

    strips = []
    for k in range(row_blocks):
        sent = response(dims, k, meta, flipped, basis, n, kernel, perturbation, quad_weight)
        strips.append([sent[0]] + [to_peer(sent[o], o) for o in range(1, n_pts)])

    inner, result = [], None
    for k in range(row_blocks):
        cut, pairs = combine(dims, k, meta, strips[: k + 1], inner)
        inner.append(pairs)
        back = across(cut)
        result = widen(dims, k * BLOCK, BLOCK, dens_blocks.shape[1], meta, back, result)
    return result, n


def solution(mesh):
    placed = (
        P(None, "pts", "mat"),
        P("mat", "pts", None),
        P("mat", "pts"),
        P("mat", "pts"),
        P("mat", "pts"),
        P("mat", "pts"),
        P("mat", "pts", None),
        P(),
    )

    return jax.shard_map(
        body,
        mesh=mesh,
        in_specs=placed,
        out_specs=(P(None, "pts", "mat"), P("mat", "pts")),
        check_vma=False,
    )
```

```python
import functools

import jax
import jax.numpy as jnp
from jax import lax
from jax.experimental import pallas as pl
from jax.experimental.pallas import tpu as pltpu
from jax.sharding import PartitionSpec as P


BLOCK = 128
VM = pl.BlockSpec(memory_space=pltpu.VMEM)
ANY = pl.BlockSpec(memory_space=pl.ANY)
HEAD = 3
GRANT = pltpu.CompilerParams(vmem_limit_bytes=20 << 20)


def cost(flops, moved):
    return pl.CostEstimate(flops=int(flops), bytes_accessed=int(moved), transcendentals=0)


def lanes(block):
    return pl.ds(pl.multiple_of(block * BLOCK, BLOCK), BLOCK)


def rows_at(block):
    return pl.ds(pl.multiple_of(block * BLOCK, BLOCK), BLOCK)


def active_rows(dims, meta, o, column):
    _, n_pts, act, nact = dims
    out = []
    for r in range(act // n_pts):
        found = jnp.int32(0)
        for j in range(nact):
            found += (meta[HEAD + o * nact + j] == column * (act // n_pts) + r).astype(jnp.int32)
        out.append(found)
    return out


def ranked_row(flags, rank, from_end):
    row, passed = jnp.int32(-1), jnp.int32(0)
    order = range(len(flags) - 1, -1, -1) if from_end else range(len(flags))
    for r in order:
        row = jnp.where((flags[r] != 0) & (passed == rank), r, row)
        passed += flags[r]
    return row


def list_slots(dims, meta, table, base, o, column, row, lower, positions):
    _, n_pts, act, nact = dims
    each = act // n_pts
    filled = jnp.int32(0)
    for j in range(nact + 1):
        table[base + j] = 0
    for j in range(nact):
        block = meta[HEAD + o * nact + j]
        local = block - column * each
        kept = (local < 0) | (local >= each) | ((local <= row) if lower else (local >= row))
        table[base + filled] = j if positions else block
        filled += kept.astype(jnp.int32)


def slots_in(dims, k):
    return dims[3] - dims[2] // dims[1] + 1 + k


def slots_out(dims, k):
    return dims[3] - k


def pack_kernel(dims, k, meta, *refs):
    n_mat, n_pts, act, nact = dims
    each = act // n_pts
    arrived, earlier = refs[:n_mat], refs[n_mat : n_mat + k]
    stage, packed, table = refs[n_mat + k], refs[n_mat + k + 1 : -1], refs[-1]
    width = arrived[0].shape[1]
    me_pts = meta[1]
    pattern_at = HEAD + n_pts * nact + (me_pts * each + k) * act
    for d in range(n_mat):
        m = meta[0] ^ d
        for c in range(width // BLOCK):
            b = m * (width // BLOCK) + c
            value = arrived[d][:, c * BLOCK : (c + 1) * BLOCK]
            stage[:, lanes(b)] = jnp.where(meta[pattern_at + b] != 0, value, jnp.zeros_like(value))
    for r in range(k):
        mine, other = me_pts * each + r, me_pts * each + k
        pair = stage[:, lanes(mine)].astype(jnp.float32) + earlier[r][:, lanes(other)].astype(jnp.float32).T
        stage[:, lanes(mine)] = pair.astype(jnp.bfloat16)
    for o in range(n_pts):
        flags = active_rows(dims, meta, o, me_pts)
        row = jnp.maximum(ranked_row(flags, each - 1 - k, True), 0)
        list_slots(dims, meta, table, o * (nact + 1), o, me_pts, row, True, False)
        for r in range(k + 1):
            source = stage if r == k else earlier[r]

            @pl.when(row == r)
            def _(source=source, o=o):
                for slot in range(slots_in(dims, k)):
                    b = table[o * (nact + 1) + slot]
                    packed[o][:, slot * BLOCK : (slot + 1) * BLOCK] = source[:, lanes(b)]


def pack(dims, k, meta, arrived, earlier):
    n_mat, n_pts, act, nact = dims
    shapes = [jax.ShapeDtypeStruct((BLOCK, act * BLOCK), jnp.bfloat16)]
    shapes += [jax.ShapeDtypeStruct((BLOCK, slots_in(dims, k) * BLOCK), jnp.bfloat16)] * n_pts
    out = pl.pallas_call(
        functools.partial(pack_kernel, dims, k),
        out_shape=shapes,
        in_specs=[pl.BlockSpec(memory_space=pltpu.SMEM)] + [VM] * (n_mat + k),
        out_specs=[VM] * len(shapes),
        scratch_shapes=[pltpu.SMEM((n_pts * (nact + 1),), jnp.int32)],
        compiler_params=GRANT,
        cost_estimate=cost(0, 2 * BLOCK * BLOCK * (act + n_pts * nact)),
    )(meta, *arrived, *earlier)
    return out[0], out[1:]


def transpose_kernel(given, out):
    out[...] = given[...].T


def transposed(basis):
    points, orbitals = basis.shape
    tile = 256
    return pl.pallas_call(
        transpose_kernel,
        out_shape=jax.ShapeDtypeStruct((orbitals, points), basis.dtype),
        grid=(points // tile,),
        in_specs=[pl.BlockSpec((tile, orbitals), lambda i: (i, 0))],
        out_specs=pl.BlockSpec((orbitals, tile), lambda i: (0, i)),
        compiler_params=GRANT,
        cost_estimate=cost(0, 4 * points * orbitals),
        name="flip",
    )(basis)


def invert(dims, meta, place):
    _, _, act, nact = dims
    for a in range(act):
        place[a] = -1
    for i in range(nact):
        place[meta[HEAD + i]] = i


def tile_of(columns, cases):
    half = columns // 2
    return half if cases <= 4 and half % BLOCK == 0 else 2 * BLOCK


def density_kernel(dims, k, tile, last, meta, *refs):
    _, n_pts, act, nact = dims
    each = act // n_pts
    parts, flipped, before, after, place, table, left = refs[:n_pts], *refs[n_pts:]
    invert(dims, meta, place)
    points = flipped.shape[1]
    rows = []
    left[...] = jnp.zeros_like(left)
    for o in range(n_pts):
        column = meta[1] ^ o
        row = ranked_row(active_rows(dims, meta, 0, column), each - 1 - k, True)
        list_slots(dims, meta, table, o * (nact + 1), 0, column, jnp.maximum(row, 0), True, True)
        rows.append((jnp.maximum(place[column * each + jnp.maximum(row, 0)], 0), row >= 0))
        for slot in range(slots_in(dims, k)):
            j = table[o * (nact + 1) + slot]
            left[o * BLOCK : (o + 1) * BLOCK, lanes(j)] = parts[o][:, slot * BLOCK : (slot + 1) * BLOCK]

    @pl.loop(0, points // tile)
    def _(t):
        at = pl.ds(pl.multiple_of(t * tile, tile), tile)
        inner = jnp.dot(left[...], flipped[:, at], preferred_element_type=jnp.float32)
        total = before[:, at]
        for o, (spot, valid) in enumerate(rows):
            own = flipped[rows_at(spot), at].astype(jnp.float32)
            share = jnp.sum(inner[o * BLOCK : (o + 1) * BLOCK] * own, axis=0, keepdims=True)
            total = total + jnp.where(valid, share, jnp.zeros_like(share))
        if last:
            point = t * tile + lax.broadcasted_iota(jnp.int32, total.shape, 1)
            total = jnp.where(point < meta[2], total, jnp.zeros_like(total))
        after[:, at] = total


def density(dims, k, last, meta, parts, flipped, before):
    _, n_pts, act, nact = dims
    orbitals, points = flipped.shape
    return pl.pallas_call(
        functools.partial(density_kernel, dims, k, tile_of(points, n_pts), last),
        out_shape=jax.ShapeDtypeStruct((1, points), jnp.float32),
        in_specs=[pl.BlockSpec(memory_space=pltpu.SMEM)] + [VM] * (n_pts + 2),
        out_specs=VM,
        scratch_shapes=[
            pltpu.SMEM((act,), jnp.int32),
            pltpu.SMEM((n_pts * (nact + 1),), jnp.int32),
            pltpu.VMEM((n_pts * BLOCK, orbitals), jnp.bfloat16),
        ],
        compiler_params=GRANT,
        cost_estimate=cost(2 * n_pts * BLOCK * orbitals * points, 2 * orbitals * points),
    )(meta, *parts, flipped, before)


def response_kernel(dims, ranks, tile, meta, *refs):
    _, n_pts, act, nact = dims
    each = act // n_pts
    flipped, basis, n, kern, pert, weight = refs[:6]
    out, (place, table, left, right) = refs[6:-4], refs[-4:]
    invert(dims, meta, place)
    points = flipped.shape[1]
    inside = lax.broadcasted_iota(jnp.int32, (1, points), 1) < meta[2]
    scaling = jnp.where(inside, weight[...] * (pert[...] - kern[...] * n[...]), 0.0)
    cases = [(k, o) for k in ranks for o in range(n_pts)]
    for at, (k, o) in enumerate(cases):
        column = meta[1] ^ o
        row = ranked_row(active_rows(dims, meta, 0, column), k, False)
        list_slots(dims, meta, table, at * (nact + 1), 0, column, jnp.maximum(row, 0), False, True)
        spot = jnp.maximum(place[column * each + jnp.maximum(row, 0)], 0)
        own = flipped[rows_at(spot), :].astype(jnp.float32)
        left[at * BLOCK : (at + 1) * BLOCK, :] = jnp.where(row >= 0, own * scaling, 0.0).astype(jnp.bfloat16)

    @pl.loop(0, basis.shape[1] // tile)
    def _(t):
        cols = pl.ds(pl.multiple_of(t * tile, tile), tile)
        right[:, cols] = jnp.dot(left[...], basis[:, cols], preferred_element_type=jnp.float32).astype(jnp.bfloat16)

    for at, (k, o) in enumerate(cases):
        for slot in range(slots_out(dims, k)):
            j = table[at * (nact + 1) + slot]
            out[at][:, slot * BLOCK : (slot + 1) * BLOCK] = right[at * BLOCK : (at + 1) * BLOCK, lanes(j)]


def response(dims, ranks, meta, flipped, basis, n, kern, pert, weight):
    _, n_pts, act, nact = dims
    orbitals, points = flipped.shape
    cases = n_pts * len(ranks)
    shapes = [
        jax.ShapeDtypeStruct((BLOCK, slots_out(dims, k) * BLOCK), jnp.bfloat16) for k in ranks for _ in range(n_pts)
    ]
    out = pl.pallas_call(
        functools.partial(response_kernel, dims, ranks, tile_of(orbitals, cases)),
        out_shape=shapes,
        in_specs=[pl.BlockSpec(memory_space=pltpu.SMEM)] + [VM] * 6,
        out_specs=[VM] * len(shapes),
        scratch_shapes=[
            pltpu.SMEM((act,), jnp.int32),
            pltpu.SMEM((cases * (nact + 1),), jnp.int32),
            pltpu.VMEM((cases * BLOCK, points), jnp.bfloat16),
            pltpu.VMEM((cases * BLOCK, orbitals), jnp.bfloat16),
        ],
        compiler_params=pltpu.CompilerParams(vmem_limit_bytes=26 << 20),
        cost_estimate=cost(2 * cases * BLOCK * orbitals * points, 4 * orbitals * points),
    )(meta, flipped, basis, n, kern, pert, weight)
    return [out[at * n_pts : (at + 1) * n_pts] for at in range(len(ranks))]


def combine_kernel(dims, k, meta, *refs):
    n_mat, n_pts, act, nact = dims
    each = act // n_pts
    strips, before = refs[: (k + 1) * n_pts], refs[(k + 1) * n_pts : (k + 1) * n_pts + k]
    out, (inner, total, table, held, sem) = refs[(k + 1) * n_pts + k : -5], refs[-5:]
    me_pts = meta[1]
    first = me_pts * each
    ranks = []
    for o in range(n_pts):
        flags = active_rows(dims, meta, o, me_pts)
        ranks.append(jnp.where(flags[k] != 0, sum(flags[:k], jnp.int32(0)), -1))
        for i in range(k + 1):

            @pl.when(ranks[o] == i)
            def _(o=o, i=i):
                filled = slots_out(dims, i) * BLOCK
                pltpu.make_async_copy(strips[i * n_pts + o], held.at[o, :, :filled], sem.at[o]).start()

        list_slots(dims, meta, table, o * (nact + 1), o, me_pts, jnp.int32(k), False, False)
    total[...] = jnp.zeros_like(total)
    for o in range(n_pts):
        for i in range(k + 1):

            @pl.when(ranks[o] == i)
            def _(o=o, i=i):
                filled = slots_out(dims, i) * BLOCK
                pltpu.make_async_copy(strips[i * n_pts + o], held.at[o, :, :filled], sem.at[o]).wait()
                for slot in range(slots_out(dims, i)):
                    b = table[o * (nact + 1) + slot]
                    part = held[o, :, slot * BLOCK : (slot + 1) * BLOCK].astype(jnp.float32)
                    total[:, lanes(b)] += part

    for r in range(k):
        total[:, lanes(first + r)] = before[r][:, k * BLOCK : (k + 1) * BLOCK].T
    for r in range(each):
        inner[:, r * BLOCK : (r + 1) * BLOCK] = total[:, lanes(first + r)]
    width = act // n_mat
    pattern_at = HEAD + n_pts * nact + (first + k) * act
    for d in range(n_mat):
        for c in range(width):
            b = (meta[0] ^ d) * width + c
            value = total[:, lanes(b)]
            value = jnp.where(meta[pattern_at + b] != 0, value, jnp.zeros_like(value))
            out[d][:, c * BLOCK : (c + 1) * BLOCK] = value.astype(jnp.bfloat16)


def combine(dims, k, meta, strips, before):
    n_mat, n_pts, act, nact = dims
    shapes = [jax.ShapeDtypeStruct((BLOCK, act // n_mat * BLOCK), jnp.bfloat16)] * n_mat
    shapes += [jax.ShapeDtypeStruct((BLOCK, act // n_pts * BLOCK), jnp.float32)]
    given = sum(strips, [])
    out = pl.pallas_call(
        functools.partial(combine_kernel, dims, k),
        out_shape=shapes,
        in_specs=[pl.BlockSpec(memory_space=pltpu.SMEM)] + [ANY] * len(given) + [VM] * k,
        out_specs=[VM] * len(shapes),
        scratch_shapes=[
            pltpu.VMEM((BLOCK, act * BLOCK), jnp.float32),
            pltpu.SMEM((n_pts * (nact + 1),), jnp.int32),
            pltpu.VMEM((n_pts, BLOCK, nact * BLOCK), jnp.bfloat16),
            pltpu.SemaphoreType.DMA((n_pts,)),
        ],
        compiler_params=GRANT,
        cost_estimate=cost(0, 2 * BLOCK * BLOCK * (act + n_pts * nact)),
    )(meta, *given, *before)
    return out[:-1], out[-1]


def widen_kernel(n_mat, meta, *refs):
    out = refs[-1]
    for d in range(n_mat):
        out[meta[0] ^ d] = refs[d][...].astype(jnp.float32)


def widen(dims, start, rows, all_rows, meta, given, held):
    n_mat, _, act, _ = dims
    width = act // n_mat * BLOCK
    more = [] if held is None else [held]
    return pl.pallas_call(
        functools.partial(widen_kernel, n_mat),
        out_shape=jax.ShapeDtypeStruct((n_mat, all_rows, width), jnp.float32),
        grid_spec=pltpu.PrefetchScalarGridSpec(
            num_scalar_prefetch=1,
            grid=(1,),
            in_specs=[pl.BlockSpec((rows, width), lambda i, meta: (0, 0))] * n_mat + [ANY] * len(more),
            out_specs=pl.BlockSpec((n_mat, rows, width), lambda i, meta: (0, start // rows, 0)),
        ),
        input_output_aliases={} if held is None else {1 + n_mat: 0},
        compiler_params=GRANT,
        cost_estimate=cost(0, 6 * rows * n_mat * width),
    )(meta, *given, *more)


def emissions(row_blocks):
    return [(0,)] + ([tuple(range(1, row_blocks))] if row_blocks > 1 else [])


def body(dens_blocks, basis_values, kernel, perturbation, quad_weight, point_count, active_blocks, block_pattern):
    n_mat, n_pts = lax.axis_size("mat"), lax.axis_size("pts")
    act, nact = block_pattern.shape[1], active_blocks.shape[2]
    dims = (n_mat, n_pts, act, nact)
    row_blocks = act // n_pts
    me_mat, me_pts = lax.axis_index("mat"), lax.axis_index("pts")

    def to_peer(value, o):
        return lax.ppermute(value, "pts", [(i, i ^ o) for i in range(n_pts)])

    points = basis_values.shape[1]
    basis = basis_values[0]
    own_active = active_blocks[0, 0]

    def across(values):
        out = [values[0]] + [None] * (n_mat - 1)
        for d in range(n_mat - 1, 0, -1):
            out[d] = lax.ppermute(values[d], "mat", [(i, i ^ d) for i in range(n_mat)])
        return out

    arrived = []
    for k in range(row_blocks):
        cut = [
            lax.dynamic_slice(dens_blocks, (me_mat ^ d, k * BLOCK, 0), (1, BLOCK, dens_blocks.shape[2]))[0]
            for d in range(n_mat)
        ]
        arrived.append(across(cut))

    peers = [own_active] + [to_peer(own_active, o) for o in range(1, n_pts)]
    pattern = lax.dynamic_index_in_dim(block_pattern, me_mat, 0, keepdims=False).reshape(-1)
    head = jnp.stack([me_mat, me_pts, point_count[0, 0]]).astype(jnp.int32)
    meta = jnp.concatenate([head] + peers + [pattern])

    flipped = transposed(basis)

    parts, stages = [], []
    for k in range(row_blocks):
        held, packed = pack(dims, k, meta, arrived[k], stages)
        stages.append(held)
        parts.append([packed[0]] + [to_peer(packed[o], o) for o in range(1, n_pts)])

    n = jnp.zeros((1, points), jnp.float32)
    for k in range(row_blocks):
        n = density(dims, k, k == row_blocks - 1, meta, parts[k], flipped, n)

    strips = []
    for ranks in emissions(row_blocks):
        several = response(dims, ranks, meta, flipped, basis, n, kernel, perturbation, quad_weight)
        for k, sent in zip(ranks, several):
            strips.append([sent[0]] + [to_peer(sent[o], o) for o in range(1, n_pts)])

    inner, result = [], None
    for k in range(row_blocks):
        cut, pairs = combine(dims, k, meta, strips[: k + 1], inner)
        inner.append(pairs)
        back = across(cut)
        result = widen(dims, k * BLOCK, BLOCK, dens_blocks.shape[1], meta, back, result)
    return result, n


def solution(mesh):
    placed = (
        P(None, "pts", "mat"),
        P("mat", "pts", None),
        P("mat", "pts"),
        P("mat", "pts"),
        P("mat", "pts"),
        P("mat", "pts"),
        P("mat", "pts", None),
        P(),
    )

    return jax.shard_map(
        body,
        mesh=mesh,
        in_specs=placed,
        out_specs=(P(None, "pts", "mat"), P("mat", "pts")),
        check_vma=False,
    )
```

```python
import functools

import jax
import jax.numpy as jnp
from jax import lax
from jax.experimental import pallas as pl
from jax.experimental.pallas import tpu as pltpu
from jax.sharding import PartitionSpec as P


BLOCK = 128
VM = pl.BlockSpec(memory_space=pltpu.VMEM)
ANY = pl.BlockSpec(memory_space=pl.ANY)
HEAD = 3
GRANT = pltpu.CompilerParams(vmem_limit_bytes=20 << 20)


def cost(flops, moved):
    return pl.CostEstimate(flops=int(flops), bytes_accessed=int(moved), transcendentals=0)


def lanes(block):
    return pl.ds(pl.multiple_of(block * BLOCK, BLOCK), BLOCK)


def rows_at(block):
    return pl.ds(pl.multiple_of(block * BLOCK, BLOCK), BLOCK)


def active_rows(dims, meta, o, column):
    _, n_pts, act, nact = dims
    out = []
    for r in range(act // n_pts):
        found = jnp.int32(0)
        for j in range(nact):
            found += (meta[HEAD + o * nact + j] == column * (act // n_pts) + r).astype(jnp.int32)
        out.append(found)
    return out


def ranked_row(flags, rank, from_end):
    row, passed = jnp.int32(-1), jnp.int32(0)
    order = range(len(flags) - 1, -1, -1) if from_end else range(len(flags))
    for r in order:
        row = jnp.where((flags[r] != 0) & (passed == rank), r, row)
        passed += flags[r]
    return row


def list_slots(dims, meta, table, base, o, column, row, lower, positions):
    _, n_pts, act, nact = dims
    each = act // n_pts
    filled = jnp.int32(0)
    for j in range(nact + 1):
        table[base + j] = 0
    for j in range(nact):
        block = meta[HEAD + o * nact + j]
        local = block - column * each
        kept = (local < 0) | (local >= each) | ((local <= row) if lower else (local >= row))
        table[base + filled] = j if positions else block
        filled += kept.astype(jnp.int32)


def slots_in(dims, k):
    return dims[3] - dims[2] // dims[1] + 1 + k


def slots_out(dims, k):
    return dims[3] - k


def pack_kernel(dims, k, pieces, meta, *refs):
    n_mat, n_pts, act, nact = dims
    each = act // n_pts
    arrived, earlier = refs[:n_mat], refs[n_mat : n_mat + k]
    stage, packed, table = refs[n_mat + k], refs[n_mat + k + 1 : -1], refs[-1]
    width = arrived[0].shape[1]
    me_pts = meta[1]
    pattern_at = HEAD + n_pts * nact + (me_pts * each + k) * act
    for d in range(n_mat):
        m = meta[0] ^ d
        for c in range(width // BLOCK):
            b = m * (width // BLOCK) + c
            value = arrived[d][:, c * BLOCK : (c + 1) * BLOCK]
            stage[:, lanes(b)] = jnp.where(meta[pattern_at + b] != 0, value, jnp.zeros_like(value))
    for r in range(k):
        mine, other = me_pts * each + r, me_pts * each + k
        pair = stage[:, lanes(mine)].astype(jnp.float32) + earlier[r][:, lanes(other)].astype(jnp.float32).T
        stage[:, lanes(mine)] = pair.astype(jnp.bfloat16)
    for o in range(n_pts):
        flags = active_rows(dims, meta, o, me_pts)
        row = jnp.maximum(ranked_row(flags, each - 1 - k, True), 0)
        list_slots(dims, meta, table, o * (nact + 1), o, me_pts, row, True, False)
        for r in range(k + 1):
            source = stage if r == k else earlier[r]

            @pl.when(row == r)
            def _(source=source, o=o):
                for slot in range(slots_in(dims, k)):
                    b = table[o * (nact + 1) + slot]
                    for h in range(pieces):
                        part = source[h * BLOCK // pieces : (h + 1) * BLOCK // pieces, lanes(b)]
                        packed[h * n_pts + o][:, slot * BLOCK : (slot + 1) * BLOCK] = part


def pack(dims, k, pieces, meta, arrived, earlier):
    n_mat, n_pts, act, nact = dims
    shapes = [jax.ShapeDtypeStruct((BLOCK, act * BLOCK), jnp.bfloat16)]
    shapes += [jax.ShapeDtypeStruct((BLOCK // pieces, slots_in(dims, k) * BLOCK), jnp.bfloat16)] * (pieces * n_pts)
    out = pl.pallas_call(
        functools.partial(pack_kernel, dims, k, pieces),
        out_shape=shapes,
        in_specs=[pl.BlockSpec(memory_space=pltpu.SMEM)] + [VM] * (n_mat + k),
        out_specs=[VM] * len(shapes),
        scratch_shapes=[pltpu.SMEM((n_pts * (nact + 1),), jnp.int32)],
        compiler_params=GRANT,
        cost_estimate=cost(0, 2 * BLOCK * BLOCK * (act + n_pts * nact)),
    )(meta, *arrived, *earlier)
    return out[0], [out[1 + h * n_pts : 1 + (h + 1) * n_pts] for h in range(pieces)]


def transpose_kernel(given, out):
    out[...] = given[...].T


def transposed(basis):
    points, orbitals = basis.shape
    tile = 256
    return pl.pallas_call(
        transpose_kernel,
        out_shape=jax.ShapeDtypeStruct((orbitals, points), basis.dtype),
        grid=(points // tile,),
        in_specs=[pl.BlockSpec((tile, orbitals), lambda i: (i, 0))],
        out_specs=pl.BlockSpec((orbitals, tile), lambda i: (0, i)),
        compiler_params=GRANT,
        cost_estimate=cost(0, 4 * points * orbitals),
        name="flip",
    )(basis)


def invert(dims, meta, place):
    _, _, act, nact = dims
    for a in range(act):
        place[a] = -1
    for i in range(nact):
        place[meta[HEAD + i]] = i


def tile_of(columns, cases):
    half = columns // 2
    return half if cases <= 4 and half % BLOCK == 0 else 2 * BLOCK


def density_kernel(dims, k, h, tile, last, meta, *refs):
    _, n_pts, act, nact = dims
    height = refs[0].shape[0]
    each = act // n_pts
    parts, flipped, before, after, place, table, left = refs[:n_pts], *refs[n_pts:]
    invert(dims, meta, place)
    points = flipped.shape[1]
    rows = []
    left[...] = jnp.zeros_like(left)
    for o in range(n_pts):
        column = meta[1] ^ o
        row = ranked_row(active_rows(dims, meta, 0, column), each - 1 - k, True)
        list_slots(dims, meta, table, o * (nact + 1), 0, column, jnp.maximum(row, 0), True, True)
        rows.append((jnp.maximum(place[column * each + jnp.maximum(row, 0)], 0), row >= 0))
        for slot in range(slots_in(dims, k)):
            j = table[o * (nact + 1) + slot]
            left[o * height : (o + 1) * height, lanes(j)] = parts[o][:, slot * BLOCK : (slot + 1) * BLOCK]

    @pl.loop(0, points // tile)
    def _(t):
        at = pl.ds(pl.multiple_of(t * tile, tile), tile)
        inner = jnp.dot(left[...], flipped[:, at], preferred_element_type=jnp.float32)
        total = before[:, at]
        for o, (spot, valid) in enumerate(rows):
            where = pl.ds(pl.multiple_of(spot * BLOCK + h * height, height), height)
            own = flipped[where, at].astype(jnp.float32)
            share = jnp.sum(inner[o * height : (o + 1) * height] * own, axis=0, keepdims=True)
            total = total + jnp.where(valid, share, jnp.zeros_like(share))
        if last:
            point = t * tile + lax.broadcasted_iota(jnp.int32, total.shape, 1)
            total = jnp.where(point < meta[2], total, jnp.zeros_like(total))
        after[:, at] = total


def density(dims, k, h, meta, parts, flipped, before):
    _, n_pts, act, nact = dims
    orbitals, points = flipped.shape
    height = parts[0].shape[0]
    return pl.pallas_call(
        functools.partial(density_kernel, dims, k, h, tile_of(points, n_pts), False),
        out_shape=jax.ShapeDtypeStruct((1, points), jnp.float32),
        in_specs=[pl.BlockSpec(memory_space=pltpu.SMEM)] + [VM] * (n_pts + 2),
        out_specs=VM,
        scratch_shapes=[
            pltpu.SMEM((act,), jnp.int32),
            pltpu.SMEM((n_pts * (nact + 1),), jnp.int32),
            pltpu.VMEM((n_pts * height, orbitals), jnp.bfloat16),
        ],
        compiler_params=GRANT,
        cost_estimate=cost(2 * n_pts * height * orbitals * points, 2 * orbitals * points),
    )(meta, *parts, flipped, before)


def turn_kernel(dims, k, h, tile, meta, *refs):
    _, n_pts, _, _ = dims
    parts, (flipped, before, basis, kern, pert, weight) = refs[:n_pts], refs[n_pts : n_pts + 6]
    out, (n, n_again, place, table, short, left, right) = refs[n_pts + 6 : -7], refs[-7:]
    density_kernel(dims, k, h, tile, True, meta, *parts, flipped, before, n, place, table, short)
    n_again[...] = n[...]
    response_kernel(dims, (0,), tile, meta, flipped, basis, n, kern, pert, weight, *out, place, table, left, right)


def turn(dims, k, h, meta, parts, flipped, before, basis, kern, pert, weight):
    _, n_pts, act, nact = dims
    orbitals, points = flipped.shape
    height = parts[0].shape[0]
    shapes = [jax.ShapeDtypeStruct((BLOCK, slots_out(dims, 0) * BLOCK), jnp.bfloat16)] * n_pts
    shapes += [jax.ShapeDtypeStruct((1, points), jnp.float32)] * 2
    out = pl.pallas_call(
        functools.partial(turn_kernel, dims, k, h, tile_of(points, n_pts)),
        out_shape=shapes,
        in_specs=[pl.BlockSpec(memory_space=pltpu.SMEM)] + [VM] * (n_pts + 6),
        out_specs=[VM] * len(shapes),
        scratch_shapes=[
            pltpu.SMEM((act,), jnp.int32),
            pltpu.SMEM((n_pts * (nact + 1),), jnp.int32),
            pltpu.VMEM((n_pts * height, orbitals), jnp.bfloat16),
            pltpu.VMEM((n_pts * BLOCK, points), jnp.bfloat16),
            pltpu.VMEM((n_pts * BLOCK, orbitals), jnp.bfloat16),
        ],
        compiler_params=pltpu.CompilerParams(vmem_limit_bytes=26 << 20),
        cost_estimate=cost(2 * n_pts * (BLOCK + height) * orbitals * points, 4 * orbitals * points),
        name="turn",
    )(meta, *parts, flipped, before, basis, kern, pert, weight)
    return out[:n_pts], out[-2], out[-1]


def response_kernel(dims, ranks, tile, meta, *refs):
    _, n_pts, act, nact = dims
    each = act // n_pts
    flipped, basis, n, kern, pert, weight = refs[:6]
    out, (place, table, left, right) = refs[6:-4], refs[-4:]
    invert(dims, meta, place)
    points = flipped.shape[1]
    inside = lax.broadcasted_iota(jnp.int32, (1, points), 1) < meta[2]
    scaling = jnp.where(inside, weight[...] * (pert[...] - kern[...] * n[...]), 0.0)
    cases = [(k, o) for k in ranks for o in range(n_pts)]
    for at, (k, o) in enumerate(cases):
        column = meta[1] ^ o
        row = ranked_row(active_rows(dims, meta, 0, column), k, False)
        list_slots(dims, meta, table, at * (nact + 1), 0, column, jnp.maximum(row, 0), False, True)
        spot = jnp.maximum(place[column * each + jnp.maximum(row, 0)], 0)
        own = flipped[rows_at(spot), :].astype(jnp.float32)
        left[at * BLOCK : (at + 1) * BLOCK, :] = jnp.where(row >= 0, own * scaling, 0.0).astype(jnp.bfloat16)

    @pl.loop(0, basis.shape[1] // tile)
    def _(t):
        cols = pl.ds(pl.multiple_of(t * tile, tile), tile)
        right[:, cols] = jnp.dot(left[...], basis[:, cols], preferred_element_type=jnp.float32).astype(jnp.bfloat16)

    for at, (k, o) in enumerate(cases):
        for slot in range(slots_out(dims, k)):
            j = table[at * (nact + 1) + slot]
            out[at][:, slot * BLOCK : (slot + 1) * BLOCK] = right[at * BLOCK : (at + 1) * BLOCK, lanes(j)]


def response(dims, ranks, meta, flipped, basis, n, kern, pert, weight):
    _, n_pts, act, nact = dims
    orbitals, points = flipped.shape
    cases = n_pts * len(ranks)
    shapes = [
        jax.ShapeDtypeStruct((BLOCK, slots_out(dims, k) * BLOCK), jnp.bfloat16) for k in ranks for _ in range(n_pts)
    ]
    out = pl.pallas_call(
        functools.partial(response_kernel, dims, ranks, tile_of(orbitals, cases)),
        out_shape=shapes,
        in_specs=[pl.BlockSpec(memory_space=pltpu.SMEM)] + [VM] * 6,
        out_specs=[VM] * len(shapes),
        scratch_shapes=[
            pltpu.SMEM((act,), jnp.int32),
            pltpu.SMEM((cases * (nact + 1),), jnp.int32),
            pltpu.VMEM((cases * BLOCK, points), jnp.bfloat16),
            pltpu.VMEM((cases * BLOCK, orbitals), jnp.bfloat16),
        ],
        compiler_params=pltpu.CompilerParams(vmem_limit_bytes=26 << 20),
        cost_estimate=cost(2 * cases * BLOCK * orbitals * points, 4 * orbitals * points),
    )(meta, flipped, basis, n, kern, pert, weight)
    return [out[at * n_pts : (at + 1) * n_pts] for at in range(len(ranks))]


def combine_kernel(dims, k, meta, *refs):
    n_mat, n_pts, act, nact = dims
    each = act // n_pts
    strips, before = refs[: (k + 1) * n_pts], refs[(k + 1) * n_pts : (k + 1) * n_pts + k]
    out, (inner, total, table, held, sem) = refs[(k + 1) * n_pts + k : -5], refs[-5:]
    me_pts = meta[1]
    first = me_pts * each
    ranks = []
    for o in range(n_pts):
        flags = active_rows(dims, meta, o, me_pts)
        ranks.append(jnp.where(flags[k] != 0, sum(flags[:k], jnp.int32(0)), -1))
        for i in range(k + 1):

            @pl.when(ranks[o] == i)
            def _(o=o, i=i):
                filled = slots_out(dims, i) * BLOCK
                pltpu.make_async_copy(strips[i * n_pts + o], held.at[o, :, :filled], sem.at[o]).start()

        list_slots(dims, meta, table, o * (nact + 1), o, me_pts, jnp.int32(k), False, False)
    total[...] = jnp.zeros_like(total)
    for o in range(n_pts):
        for i in range(k + 1):

            @pl.when(ranks[o] == i)
            def _(o=o, i=i):
                filled = slots_out(dims, i) * BLOCK
                pltpu.make_async_copy(strips[i * n_pts + o], held.at[o, :, :filled], sem.at[o]).wait()
                for slot in range(slots_out(dims, i)):
                    b = table[o * (nact + 1) + slot]
                    part = held[o, :, slot * BLOCK : (slot + 1) * BLOCK].astype(jnp.float32)
                    total[:, lanes(b)] += part

    for r in range(k):
        total[:, lanes(first + r)] = before[r][:, k * BLOCK : (k + 1) * BLOCK].T
    for r in range(each):
        inner[:, r * BLOCK : (r + 1) * BLOCK] = total[:, lanes(first + r)]
    width = act // n_mat
    pattern_at = HEAD + n_pts * nact + (first + k) * act
    for d in range(n_mat):
        for c in range(width):
            b = (meta[0] ^ d) * width + c
            value = total[:, lanes(b)]
            value = jnp.where(meta[pattern_at + b] != 0, value, jnp.zeros_like(value))
            out[d][:, c * BLOCK : (c + 1) * BLOCK] = value.astype(jnp.bfloat16)


def combine(dims, k, meta, strips, before):
    n_mat, n_pts, act, nact = dims
    shapes = [jax.ShapeDtypeStruct((BLOCK, act // n_mat * BLOCK), jnp.bfloat16)] * n_mat
    shapes += [jax.ShapeDtypeStruct((BLOCK, act // n_pts * BLOCK), jnp.float32)]
    given = sum(strips, [])
    out = pl.pallas_call(
        functools.partial(combine_kernel, dims, k),
        out_shape=shapes,
        in_specs=[pl.BlockSpec(memory_space=pltpu.SMEM)] + [ANY] * len(given) + [VM] * k,
        out_specs=[VM] * len(shapes),
        scratch_shapes=[
            pltpu.VMEM((BLOCK, act * BLOCK), jnp.float32),
            pltpu.SMEM((n_pts * (nact + 1),), jnp.int32),
            pltpu.VMEM((n_pts, BLOCK, nact * BLOCK), jnp.bfloat16),
            pltpu.SemaphoreType.DMA((n_pts,)),
        ],
        compiler_params=GRANT,
        cost_estimate=cost(0, 2 * BLOCK * BLOCK * (act + n_pts * nact)),
    )(meta, *given, *before)
    return out[:-1], out[-1]


def widen_kernel(n_mat, meta, *refs):
    out = refs[-1]
    for d in range(n_mat):
        out[meta[0] ^ d] = refs[d][...].astype(jnp.float32)


def widen(dims, start, rows, all_rows, meta, given, held):
    n_mat, _, act, _ = dims
    width = act // n_mat * BLOCK
    more = [] if held is None else [held]
    return pl.pallas_call(
        functools.partial(widen_kernel, n_mat),
        out_shape=jax.ShapeDtypeStruct((n_mat, all_rows, width), jnp.float32),
        grid_spec=pltpu.PrefetchScalarGridSpec(
            num_scalar_prefetch=1,
            grid=(1,),
            in_specs=[pl.BlockSpec((rows, width), lambda i, meta: (0, 0))] * n_mat + [ANY] * len(more),
            out_specs=pl.BlockSpec((n_mat, rows, width), lambda i, meta: (0, start // rows, 0)),
        ),
        input_output_aliases={} if held is None else {1 + n_mat: 0},
        compiler_params=GRANT,
        cost_estimate=cost(0, 6 * rows * n_mat * width),
    )(meta, *given, *more)


def pieces_of(k, row_blocks):
    return 2 if k == row_blocks - 1 else 1


def body(dens_blocks, basis_values, kernel, perturbation, quad_weight, point_count, active_blocks, block_pattern):
    n_mat, n_pts = lax.axis_size("mat"), lax.axis_size("pts")
    act, nact = block_pattern.shape[1], active_blocks.shape[2]
    dims = (n_mat, n_pts, act, nact)
    row_blocks = act // n_pts
    me_mat, me_pts = lax.axis_index("mat"), lax.axis_index("pts")

    def to_peer(value, o):
        return lax.ppermute(value, "pts", [(i, i ^ o) for i in range(n_pts)])

    points = basis_values.shape[1]
    basis = basis_values[0]
    own_active = active_blocks[0, 0]

    def across(values):
        out = [values[0]] + [None] * (n_mat - 1)
        for d in range(n_mat - 1, 0, -1):
            out[d] = lax.ppermute(values[d], "mat", [(i, i ^ d) for i in range(n_mat)])
        return out

    arrived = []
    for k in range(row_blocks):
        cut = [
            lax.dynamic_slice(dens_blocks, (me_mat ^ d, k * BLOCK, 0), (1, BLOCK, dens_blocks.shape[2]))[0]
            for d in range(n_mat)
        ]
        arrived.append(across(cut))

    peers = [own_active] + [to_peer(own_active, o) for o in range(1, n_pts)]
    pattern = lax.dynamic_index_in_dim(block_pattern, me_mat, 0, keepdims=False).reshape(-1)
    head = jnp.stack([me_mat, me_pts, point_count[0, 0]]).astype(jnp.int32)
    meta = jnp.concatenate([head] + peers + [pattern])

    flipped = transposed(basis)

    parts, stages = [], []
    for k in range(row_blocks):
        held, packed = pack(dims, k, pieces_of(k, row_blocks), meta, arrived[k], stages)
        stages.append(held)
        for h, piece in enumerate(packed):
            parts.append((k, h, [piece[0]] + [to_peer(piece[o], o) for o in range(1, n_pts)]))

    n = jnp.zeros((1, points), jnp.float32)
    for k, h, piece in parts[:-1]:
        n = density(dims, k, h, meta, piece, flipped, n)
    k, h, piece = parts[-1]
    sent, n, n_response = turn(dims, k, h, meta, piece, flipped, n, basis, kernel, perturbation, quad_weight)
    emitted = [sent]

    strips = []
    for k in range(row_blocks):
        if k == 1:
            later = tuple(range(1, row_blocks))
            emitted += response(dims, later, meta, flipped, basis, n, kernel, perturbation, quad_weight)
        strips.append([emitted[k][0]] + [to_peer(emitted[k][o], o) for o in range(1, n_pts)])

    inner, result = [], None
    for k in range(row_blocks):
        cut, pairs = combine(dims, k, meta, strips[: k + 1], inner)
        inner.append(pairs)
        back = across(cut)
        result = widen(dims, k * BLOCK, BLOCK, dens_blocks.shape[1], meta, back, result)
    return result, n_response


def solution(mesh):
    placed = (
        P(None, "pts", "mat"),
        P("mat", "pts", None),
        P("mat", "pts"),
        P("mat", "pts"),
        P("mat", "pts"),
        P("mat", "pts"),
        P("mat", "pts", None),
        P(),
    )

    return jax.shard_map(
        body,
        mesh=mesh,
        in_specs=placed,
        out_specs=(P(None, "pts", "mat"), P("mat", "pts")),
        check_vma=False,
    )
```

```python
import functools

import jax
import jax.numpy as jnp
from jax import lax
from jax.experimental import pallas as pl
from jax.experimental.pallas import tpu as pltpu
from jax.sharding import PartitionSpec as P


BLOCK = 128
VM = pl.BlockSpec(memory_space=pltpu.VMEM)
ANY = pl.BlockSpec(memory_space=pl.ANY)
HEAD = 3
GRANT = pltpu.CompilerParams(vmem_limit_bytes=20 << 20)


def cost(flops, moved):
    return pl.CostEstimate(flops=int(flops), bytes_accessed=int(moved), transcendentals=0)


def lanes(block):
    return pl.ds(pl.multiple_of(block * BLOCK, BLOCK), BLOCK)


def rows_at(block):
    return pl.ds(pl.multiple_of(block * BLOCK, BLOCK), BLOCK)


def active_rows(dims, meta, o, column):
    _, n_pts, act, nact = dims
    out = []
    for r in range(act // n_pts):
        found = jnp.int32(0)
        for j in range(nact):
            found += (meta[HEAD + o * nact + j] == column * (act // n_pts) + r).astype(jnp.int32)
        out.append(found)
    return out


def ranked_row(flags, rank, from_end):
    row, passed = jnp.int32(-1), jnp.int32(0)
    order = range(len(flags) - 1, -1, -1) if from_end else range(len(flags))
    for r in order:
        row = jnp.where((flags[r] != 0) & (passed == rank), r, row)
        passed += flags[r]
    return row


def list_slots(dims, meta, table, base, o, column, row, lower, positions):
    _, n_pts, act, nact = dims
    each = act // n_pts
    filled = jnp.int32(0)
    for j in range(nact + 1):
        table[base + j] = 0
    for j in range(nact):
        block = meta[HEAD + o * nact + j]
        local = block - column * each
        kept = (local < 0) | (local >= each) | ((local <= row) if lower else (local >= row))
        table[base + filled] = j if positions else block
        filled += kept.astype(jnp.int32)


def slots_in(dims, k):
    return dims[3] - dims[2] // dims[1] + 1 + k


def slots_out(dims, k):
    return dims[3] - k


def pack_kernel(dims, k, pieces, meta, *refs):
    n_mat, n_pts, act, nact = dims
    each = act // n_pts
    arrived, earlier = refs[:n_mat], refs[n_mat : n_mat + k]
    stage, packed, table = refs[n_mat + k], refs[n_mat + k + 1 : -1], refs[-1]
    width = arrived[0].shape[1]
    me_pts = meta[1]
    pattern_at = HEAD + n_pts * nact + (me_pts * each + k) * act
    for d in range(n_mat):
        m = meta[0] ^ d
        for c in range(width // BLOCK):
            b = m * (width // BLOCK) + c
            value = arrived[d][:, c * BLOCK : (c + 1) * BLOCK]
            stage[:, lanes(b)] = jnp.where(meta[pattern_at + b] != 0, value, jnp.zeros_like(value))
    for r in range(k):
        mine, other = me_pts * each + r, me_pts * each + k
        pair = stage[:, lanes(mine)].astype(jnp.float32) + earlier[r][:, lanes(other)].astype(jnp.float32).T
        stage[:, lanes(mine)] = pair.astype(jnp.bfloat16)
    for o in range(n_pts):
        flags = active_rows(dims, meta, o, me_pts)
        row = jnp.maximum(ranked_row(flags, each - 1 - k, True), 0)
        list_slots(dims, meta, table, o * (nact + 1), o, me_pts, row, True, False)
        for r in range(k + 1):
            source = stage if r == k else earlier[r]

            @pl.when(row == r)
            def _(source=source, o=o):
                for slot in range(slots_in(dims, k)):
                    b = table[o * (nact + 1) + slot]
                    for h in range(pieces):
                        part = source[h * BLOCK // pieces : (h + 1) * BLOCK // pieces, lanes(b)]
                        packed[h * n_pts + o][:, slot * BLOCK : (slot + 1) * BLOCK] = part


def pack(dims, k, pieces, meta, arrived, earlier):
    n_mat, n_pts, act, nact = dims
    shapes = [jax.ShapeDtypeStruct((BLOCK, act * BLOCK), jnp.bfloat16)]
    shapes += [jax.ShapeDtypeStruct((BLOCK // pieces, slots_in(dims, k) * BLOCK), jnp.bfloat16)] * (pieces * n_pts)
    out = pl.pallas_call(
        functools.partial(pack_kernel, dims, k, pieces),
        out_shape=shapes,
        in_specs=[pl.BlockSpec(memory_space=pltpu.SMEM)] + [VM] * (n_mat + k),
        out_specs=[VM] * len(shapes),
        scratch_shapes=[pltpu.SMEM((n_pts * (nact + 1),), jnp.int32)],
        compiler_params=GRANT,
        cost_estimate=cost(0, 2 * BLOCK * BLOCK * (act + n_pts * nact)),
    )(meta, *arrived, *earlier)
    return out[0], [out[1 + h * n_pts : 1 + (h + 1) * n_pts] for h in range(pieces)]


def transpose_kernel(tile, given, out, held, sem):
    pieces = given.shape[0] // tile

    def copy(i):
        at = pl.ds(pl.multiple_of(i * tile, tile), tile)
        return pltpu.make_async_copy(given.at[at], held.at[at], sem.at[i])

    for i in range(pieces):
        copy(i).start()

    @pl.loop(0, pieces)
    def _(i):
        copy(i).wait()
        at = pl.ds(pl.multiple_of(i * tile, tile), tile)
        out[:, at] = held[at, :].T


def transposed(basis):
    points, orbitals = basis.shape
    tile = 2 * BLOCK
    return pl.pallas_call(
        functools.partial(transpose_kernel, tile),
        out_shape=jax.ShapeDtypeStruct((orbitals, points), basis.dtype),
        in_specs=[pl.BlockSpec(memory_space=pltpu.HBM)],
        out_specs=VM,
        scratch_shapes=[pltpu.VMEM((points, orbitals), basis.dtype), pltpu.SemaphoreType.DMA((points // tile,))],
        compiler_params=GRANT,
        cost_estimate=cost(0, 4 * points * orbitals),
        name="flip",
    )(basis)


def invert(dims, meta, place):
    _, _, act, nact = dims
    for a in range(act):
        place[a] = -1
    for i in range(nact):
        place[meta[HEAD + i]] = i


def tile_of(columns, cases):
    half = columns // 2
    return half if cases <= 4 and half % BLOCK == 0 else 2 * BLOCK


def density_kernel(dims, k, h, tile, last, meta, *refs):
    _, n_pts, act, nact = dims
    height = refs[0].shape[0]
    each = act // n_pts
    parts, flipped, before, after, place, table, left = refs[:n_pts], *refs[n_pts:]
    invert(dims, meta, place)
    points = flipped.shape[1]
    rows = []
    left[...] = jnp.zeros_like(left)
    for o in range(n_pts):
        column = meta[1] ^ o
        row = ranked_row(active_rows(dims, meta, 0, column), each - 1 - k, True)
        list_slots(dims, meta, table, o * (nact + 1), 0, column, jnp.maximum(row, 0), True, True)
        rows.append((jnp.maximum(place[column * each + jnp.maximum(row, 0)], 0), row >= 0))
        for slot in range(slots_in(dims, k)):
            j = table[o * (nact + 1) + slot]
            left[o * height : (o + 1) * height, lanes(j)] = parts[o][:, slot * BLOCK : (slot + 1) * BLOCK]

    @pl.loop(0, points // tile)
    def _(t):
        at = pl.ds(pl.multiple_of(t * tile, tile), tile)
        inner = jnp.dot(left[...], flipped[:, at], preferred_element_type=jnp.float32)
        total = before[:, at]
        for o, (spot, valid) in enumerate(rows):
            where = pl.ds(pl.multiple_of(spot * BLOCK + h * height, height), height)
            own = flipped[where, at].astype(jnp.float32)
            share = jnp.sum(inner[o * height : (o + 1) * height] * own, axis=0, keepdims=True)
            total = total + jnp.where(valid, share, jnp.zeros_like(share))
        if last:
            point = t * tile + lax.broadcasted_iota(jnp.int32, total.shape, 1)
            total = jnp.where(point < meta[2], total, jnp.zeros_like(total))
        after[:, at] = total


def density(dims, k, h, meta, parts, flipped, before):
    _, n_pts, act, nact = dims
    orbitals, points = flipped.shape
    height = parts[0].shape[0]
    return pl.pallas_call(
        functools.partial(density_kernel, dims, k, h, tile_of(points, n_pts), False),
        out_shape=jax.ShapeDtypeStruct((1, points), jnp.float32),
        in_specs=[pl.BlockSpec(memory_space=pltpu.SMEM)] + [VM] * (n_pts + 2),
        out_specs=VM,
        scratch_shapes=[
            pltpu.SMEM((act,), jnp.int32),
            pltpu.SMEM((n_pts * (nact + 1),), jnp.int32),
            pltpu.VMEM((n_pts * height, orbitals), jnp.bfloat16),
        ],
        compiler_params=GRANT,
        cost_estimate=cost(2 * n_pts * height * orbitals * points, 2 * orbitals * points),
    )(meta, *parts, flipped, before)


def turn_kernel(dims, k, h, tile, meta, *refs):
    _, n_pts, _, _ = dims
    parts, (flipped, before, basis, kern, pert, weight) = refs[:n_pts], refs[n_pts : n_pts + 6]
    out, (n, n_again, place, table, short, left, right) = refs[n_pts + 6 : -7], refs[-7:]
    density_kernel(dims, k, h, tile, True, meta, *parts, flipped, before, n, place, table, short)
    n_again[...] = n[...]
    response_kernel(dims, (0,), tile, meta, flipped, basis, n, kern, pert, weight, *out, place, table, left, right)


def turn(dims, k, h, meta, parts, flipped, before, basis, kern, pert, weight):
    _, n_pts, act, nact = dims
    orbitals, points = flipped.shape
    height = parts[0].shape[0]
    shapes = [jax.ShapeDtypeStruct((BLOCK, slots_out(dims, 0) * BLOCK), jnp.bfloat16)] * n_pts
    shapes += [jax.ShapeDtypeStruct((1, points), jnp.float32)] * 2
    out = pl.pallas_call(
        functools.partial(turn_kernel, dims, k, h, tile_of(points, n_pts)),
        out_shape=shapes,
        in_specs=[pl.BlockSpec(memory_space=pltpu.SMEM)] + [VM] * (n_pts + 6),
        out_specs=[VM] * len(shapes),
        scratch_shapes=[
            pltpu.SMEM((act,), jnp.int32),
            pltpu.SMEM((n_pts * (nact + 1),), jnp.int32),
            pltpu.VMEM((n_pts * height, orbitals), jnp.bfloat16),
            pltpu.VMEM((n_pts * BLOCK, points), jnp.bfloat16),
            pltpu.VMEM((n_pts * BLOCK, orbitals), jnp.bfloat16),
        ],
        compiler_params=pltpu.CompilerParams(vmem_limit_bytes=26 << 20),
        cost_estimate=cost(2 * n_pts * (BLOCK + height) * orbitals * points, 4 * orbitals * points),
        name="turn",
    )(meta, *parts, flipped, before, basis, kern, pert, weight)
    return out[:n_pts], out[-2], out[-1]


def response_kernel(dims, ranks, tile, meta, *refs):
    _, n_pts, act, nact = dims
    each = act // n_pts
    flipped, basis, n, kern, pert, weight = refs[:6]
    out, (place, table, left, right) = refs[6:-4], refs[-4:]
    invert(dims, meta, place)
    points = flipped.shape[1]
    inside = lax.broadcasted_iota(jnp.int32, (1, points), 1) < meta[2]
    scaling = jnp.where(inside, weight[...] * (pert[...] - kern[...] * n[...]), 0.0)
    cases = [(k, o) for k in ranks for o in range(n_pts)]
    for at, (k, o) in enumerate(cases):
        column = meta[1] ^ o
        row = ranked_row(active_rows(dims, meta, 0, column), k, False)
        list_slots(dims, meta, table, at * (nact + 1), 0, column, jnp.maximum(row, 0), False, True)
        spot = jnp.maximum(place[column * each + jnp.maximum(row, 0)], 0)
        own = flipped[rows_at(spot), :].astype(jnp.float32)
        left[at * BLOCK : (at + 1) * BLOCK, :] = jnp.where(row >= 0, own * scaling, 0.0).astype(jnp.bfloat16)

    @pl.loop(0, basis.shape[1] // tile)
    def _(t):
        cols = pl.ds(pl.multiple_of(t * tile, tile), tile)
        right[:, cols] = jnp.dot(left[...], basis[:, cols], preferred_element_type=jnp.float32).astype(jnp.bfloat16)

    for at, (k, o) in enumerate(cases):
        for slot in range(slots_out(dims, k)):
            j = table[at * (nact + 1) + slot]
            out[at][:, slot * BLOCK : (slot + 1) * BLOCK] = right[at * BLOCK : (at + 1) * BLOCK, lanes(j)]


def response(dims, ranks, meta, flipped, basis, n, kern, pert, weight):
    _, n_pts, act, nact = dims
    orbitals, points = flipped.shape
    cases = n_pts * len(ranks)
    shapes = [
        jax.ShapeDtypeStruct((BLOCK, slots_out(dims, k) * BLOCK), jnp.bfloat16) for k in ranks for _ in range(n_pts)
    ]
    out = pl.pallas_call(
        functools.partial(response_kernel, dims, ranks, tile_of(orbitals, cases)),
        out_shape=shapes,
        in_specs=[pl.BlockSpec(memory_space=pltpu.SMEM)] + [VM] * 6,
        out_specs=[VM] * len(shapes),
        scratch_shapes=[
            pltpu.SMEM((act,), jnp.int32),
            pltpu.SMEM((cases * (nact + 1),), jnp.int32),
            pltpu.VMEM((cases * BLOCK, points), jnp.bfloat16),
            pltpu.VMEM((cases * BLOCK, orbitals), jnp.bfloat16),
        ],
        compiler_params=pltpu.CompilerParams(vmem_limit_bytes=26 << 20),
        cost_estimate=cost(2 * cases * BLOCK * orbitals * points, 4 * orbitals * points),
    )(meta, flipped, basis, n, kern, pert, weight)
    return [out[at * n_pts : (at + 1) * n_pts] for at in range(len(ranks))]


def combine_kernel(dims, k, meta, *refs):
    n_mat, n_pts, act, nact = dims
    each = act // n_pts
    strips, before = refs[: (k + 1) * n_pts], refs[(k + 1) * n_pts : (k + 1) * n_pts + k]
    out, (inner, total, table, held, sem) = refs[(k + 1) * n_pts + k : -5], refs[-5:]
    me_pts = meta[1]
    first = me_pts * each
    ranks = []
    for o in range(n_pts):
        flags = active_rows(dims, meta, o, me_pts)
        ranks.append(jnp.where(flags[k] != 0, sum(flags[:k], jnp.int32(0)), -1))
        for i in range(k + 1):

            @pl.when(ranks[o] == i)
            def _(o=o, i=i):
                filled = slots_out(dims, i) * BLOCK
                pltpu.make_async_copy(strips[i * n_pts + o], held.at[o, :, :filled], sem.at[o]).start()

        list_slots(dims, meta, table, o * (nact + 1), o, me_pts, jnp.int32(k), False, False)
    total[...] = jnp.zeros_like(total)
    for o in range(n_pts):
        for i in range(k + 1):

            @pl.when(ranks[o] == i)
            def _(o=o, i=i):
                filled = slots_out(dims, i) * BLOCK
                pltpu.make_async_copy(strips[i * n_pts + o], held.at[o, :, :filled], sem.at[o]).wait()
                for slot in range(slots_out(dims, i)):
                    b = table[o * (nact + 1) + slot]
                    part = held[o, :, slot * BLOCK : (slot + 1) * BLOCK].astype(jnp.float32)
                    total[:, lanes(b)] += part

    for r in range(k):
        total[:, lanes(first + r)] = before[r][:, k * BLOCK : (k + 1) * BLOCK].T
    for r in range(each):
        inner[:, r * BLOCK : (r + 1) * BLOCK] = total[:, lanes(first + r)]
    width = act // n_mat
    pattern_at = HEAD + n_pts * nact + (first + k) * act
    for d in range(n_mat):
        for c in range(width):
            b = (meta[0] ^ d) * width + c
            value = total[:, lanes(b)]
            value = jnp.where(meta[pattern_at + b] != 0, value, jnp.zeros_like(value))
            out[d][:, c * BLOCK : (c + 1) * BLOCK] = value.astype(jnp.bfloat16)


def combine(dims, k, meta, strips, before):
    n_mat, n_pts, act, nact = dims
    shapes = [jax.ShapeDtypeStruct((BLOCK, act // n_mat * BLOCK), jnp.bfloat16)] * n_mat
    shapes += [jax.ShapeDtypeStruct((BLOCK, act // n_pts * BLOCK), jnp.float32)]
    given = sum(strips, [])
    out = pl.pallas_call(
        functools.partial(combine_kernel, dims, k),
        out_shape=shapes,
        in_specs=[pl.BlockSpec(memory_space=pltpu.SMEM)] + [ANY] * len(given) + [VM] * k,
        out_specs=[VM] * len(shapes),
        scratch_shapes=[
            pltpu.VMEM((BLOCK, act * BLOCK), jnp.float32),
            pltpu.SMEM((n_pts * (nact + 1),), jnp.int32),
            pltpu.VMEM((n_pts, BLOCK, nact * BLOCK), jnp.bfloat16),
            pltpu.SemaphoreType.DMA((n_pts,)),
        ],
        compiler_params=GRANT,
        cost_estimate=cost(0, 2 * BLOCK * BLOCK * (act + n_pts * nact)),
    )(meta, *given, *before)
    return out[:-1], out[-1]


def widen_kernel(n_mat, meta, *refs):
    out = refs[-1]
    for d in range(n_mat):
        out[meta[0] ^ d] = refs[d][...].astype(jnp.float32)


def widen(dims, start, rows, all_rows, meta, given, held):
    n_mat, _, act, _ = dims
    width = act // n_mat * BLOCK
    more = [] if held is None else [held]
    return pl.pallas_call(
        functools.partial(widen_kernel, n_mat),
        out_shape=jax.ShapeDtypeStruct((n_mat, all_rows, width), jnp.float32),
        grid_spec=pltpu.PrefetchScalarGridSpec(
            num_scalar_prefetch=1,
            grid=(1,),
            in_specs=[pl.BlockSpec((rows, width), lambda i, meta: (0, 0))] * n_mat + [ANY] * len(more),
            out_specs=pl.BlockSpec((n_mat, rows, width), lambda i, meta: (0, start // rows, 0)),
        ),
        input_output_aliases={} if held is None else {1 + n_mat: 0},
        compiler_params=GRANT,
        cost_estimate=cost(0, 6 * rows * n_mat * width),
    )(meta, *given, *more)


def pieces_of(k, row_blocks):
    return 2 if k == row_blocks - 1 else 1


def body(dens_blocks, basis_values, kernel, perturbation, quad_weight, point_count, active_blocks, block_pattern):
    n_mat, n_pts = lax.axis_size("mat"), lax.axis_size("pts")
    act, nact = block_pattern.shape[1], active_blocks.shape[2]
    dims = (n_mat, n_pts, act, nact)
    row_blocks = act // n_pts
    me_mat, me_pts = lax.axis_index("mat"), lax.axis_index("pts")

    def to_peer(value, o):
        return lax.ppermute(value, "pts", [(i, i ^ o) for i in range(n_pts)])

    points = basis_values.shape[1]
    basis = basis_values[0]
    own_active = active_blocks[0, 0]

    def across(values):
        out = [values[0]] + [None] * (n_mat - 1)
        for d in range(n_mat - 1, 0, -1):
            out[d] = lax.ppermute(values[d], "mat", [(i, i ^ d) for i in range(n_mat)])
        return out

    arrived = []
    for k in range(row_blocks):
        cut = [
            lax.dynamic_slice(dens_blocks, (me_mat ^ d, k * BLOCK, 0), (1, BLOCK, dens_blocks.shape[2]))[0]
            for d in range(n_mat)
        ]
        arrived.append(across(cut))

    peers = [own_active] + [to_peer(own_active, o) for o in range(1, n_pts)]
    pattern = lax.dynamic_index_in_dim(block_pattern, me_mat, 0, keepdims=False).reshape(-1)
    head = jnp.stack([me_mat, me_pts, point_count[0, 0]]).astype(jnp.int32)
    meta = jnp.concatenate([head] + peers + [pattern])

    flipped = transposed(pltpu.with_memory_space_constraint(basis, pltpu.HBM))

    parts, stages = [], []
    for k in range(row_blocks):
        held, packed = pack(dims, k, pieces_of(k, row_blocks), meta, arrived[k], stages)
        stages.append(held)
        for h, piece in enumerate(packed):
            parts.append((k, h, [piece[0]] + [to_peer(piece[o], o) for o in range(1, n_pts)]))

    n = jnp.zeros((1, points), jnp.float32)
    for k, h, piece in parts[:-1]:
        n = density(dims, k, h, meta, piece, flipped, n)
    k, h, piece = parts[-1]
    sent, n, n_response = turn(dims, k, h, meta, piece, flipped, n, basis, kernel, perturbation, quad_weight)
    emitted = [sent]

    strips = []
    for k in range(row_blocks):
        if k == 1:
            later = tuple(range(1, row_blocks))
            emitted += response(dims, later, meta, flipped, basis, n, kernel, perturbation, quad_weight)
        strips.append([emitted[k][0]] + [to_peer(emitted[k][o], o) for o in range(1, n_pts)])

    inner, result = [], None
    for k in range(row_blocks):
        cut, pairs = combine(dims, k, meta, strips[: k + 1], inner)
        inner.append(pairs)
        back = across(cut)
        result = widen(dims, k * BLOCK, BLOCK, dens_blocks.shape[1], meta, back, result)
    return result, n_response


def solution(mesh):
    placed = (
        P(None, "pts", "mat"),
        P("mat", "pts", None),
        P("mat", "pts"),
        P("mat", "pts"),
        P("mat", "pts"),
        P("mat", "pts"),
        P("mat", "pts", None),
        P(),
    )

    return jax.shard_map(
        body,
        mesh=mesh,
        in_specs=placed,
        out_specs=(P(None, "pts", "mat"), P("mat", "pts")),
        check_vma=False,
    )
```

```python
import functools

import jax
import jax.numpy as jnp
from jax import lax
from jax.experimental import pallas as pl
from jax.experimental.pallas import tpu as pltpu
from jax.sharding import PartitionSpec as P


BLOCK = 128
VM = pl.BlockSpec(memory_space=pltpu.VMEM)
ANY = pl.BlockSpec(memory_space=pl.ANY)
HEAD = 3
GRANT = pltpu.CompilerParams(vmem_limit_bytes=20 << 20)


def cost(flops, moved):
    return pl.CostEstimate(flops=int(flops), bytes_accessed=int(moved), transcendentals=0)


def lanes(block):
    return pl.ds(pl.multiple_of(block * BLOCK, BLOCK), BLOCK)


def rows_at(block):
    return pl.ds(pl.multiple_of(block * BLOCK, BLOCK), BLOCK)


def active_rows(dims, meta, o, column):
    _, n_pts, act, nact = dims
    out = []
    for r in range(act // n_pts):
        found = jnp.int32(0)
        for j in range(nact):
            found += (meta[HEAD + o * nact + j] == column * (act // n_pts) + r).astype(jnp.int32)
        out.append(found)
    return out


def ranked_row(flags, rank, from_end):
    row, passed = jnp.int32(-1), jnp.int32(0)
    order = range(len(flags) - 1, -1, -1) if from_end else range(len(flags))
    for r in order:
        row = jnp.where((flags[r] != 0) & (passed == rank), r, row)
        passed += flags[r]
    return row


def list_slots(dims, meta, table, base, o, column, row, lower, positions):
    _, n_pts, act, nact = dims
    each = act // n_pts
    filled = jnp.int32(0)
    for j in range(nact + 1):
        table[base + j] = 0
    for j in range(nact):
        block = meta[HEAD + o * nact + j]
        local = block - column * each
        kept = (local < 0) | (local >= each) | ((local <= row) if lower else (local >= row))
        table[base + filled] = j if positions else block
        filled += kept.astype(jnp.int32)


def slots_in(dims, k):
    return dims[3] - dims[2] // dims[1] + 1 + k


def slots_out(dims, k):
    return dims[3] - k


def pack_kernel(dims, k, pieces, meta, *refs):
    n_mat, n_pts, act, nact = dims
    each = act // n_pts
    arrived, earlier = refs[:n_mat], refs[n_mat : n_mat + k]
    stage, packed, table = refs[n_mat + k], refs[n_mat + k + 1 : -1], refs[-1]
    width = arrived[0].shape[1]
    me_pts = meta[1]
    pattern_at = HEAD + n_pts * nact + (me_pts * each + k) * act
    for d in range(n_mat):
        m = meta[0] ^ d
        for c in range(width // BLOCK):
            b = m * (width // BLOCK) + c
            value = arrived[d][:, c * BLOCK : (c + 1) * BLOCK]
            stage[:, lanes(b)] = jnp.where(meta[pattern_at + b] != 0, value, jnp.zeros_like(value))
    for r in range(k):
        mine, other = me_pts * each + r, me_pts * each + k
        pair = stage[:, lanes(mine)].astype(jnp.float32) + earlier[r][:, lanes(other)].astype(jnp.float32).T
        stage[:, lanes(mine)] = pair.astype(jnp.bfloat16)
    for o in range(n_pts):
        flags = active_rows(dims, meta, o, me_pts)
        row = jnp.maximum(ranked_row(flags, each - 1 - k, True), 0)
        list_slots(dims, meta, table, o * (nact + 1), o, me_pts, row, True, False)
        for r in range(k + 1):
            source = stage if r == k else earlier[r]

            @pl.when(row == r)
            def _(source=source, o=o):
                for slot in range(slots_in(dims, k)):
                    b = table[o * (nact + 1) + slot]
                    for h in range(pieces):
                        part = source[h * BLOCK // pieces : (h + 1) * BLOCK // pieces, lanes(b)]
                        packed[h * n_pts + o][:, slot * BLOCK : (slot + 1) * BLOCK] = part


def pack(dims, k, pieces, meta, arrived, earlier):
    n_mat, n_pts, act, nact = dims
    shapes = [jax.ShapeDtypeStruct((BLOCK, act * BLOCK), jnp.bfloat16)]
    shapes += [jax.ShapeDtypeStruct((BLOCK // pieces, slots_in(dims, k) * BLOCK), jnp.bfloat16)] * (pieces * n_pts)
    out = pl.pallas_call(
        functools.partial(pack_kernel, dims, k, pieces),
        out_shape=shapes,
        in_specs=[pl.BlockSpec(memory_space=pltpu.SMEM)] + [VM] * (n_mat + k),
        out_specs=[VM] * len(shapes),
        scratch_shapes=[pltpu.SMEM((n_pts * (nact + 1),), jnp.int32)],
        compiler_params=GRANT,
        cost_estimate=cost(0, 2 * BLOCK * BLOCK * (act + n_pts * nact)),
    )(meta, *arrived, *earlier)
    return out[0], [out[1 + h * n_pts : 1 + (h + 1) * n_pts] for h in range(pieces)]


def transpose_kernel(tile, given, out, held, sem):
    pieces = given.shape[0] // tile

    def copy(i):
        at = pl.ds(pl.multiple_of(i * tile, tile), tile)
        return pltpu.make_async_copy(given.at[at], held.at[at], sem.at[i])

    for i in range(pieces):
        copy(i).start()

    @pl.loop(0, pieces)
    def _(i):
        copy(i).wait()
        at = pl.ds(pl.multiple_of(i * tile, tile), tile)
        out[:, at] = held[at, :].T


def transposed(basis):
    points, orbitals = basis.shape
    tile = 2 * BLOCK
    return pl.pallas_call(
        functools.partial(transpose_kernel, tile),
        out_shape=jax.ShapeDtypeStruct((orbitals, points), basis.dtype),
        in_specs=[pl.BlockSpec(memory_space=pltpu.HBM)],
        out_specs=VM,
        scratch_shapes=[pltpu.VMEM((points, orbitals), basis.dtype), pltpu.SemaphoreType.DMA((points // tile,))],
        compiler_params=GRANT,
        cost_estimate=cost(0, 4 * points * orbitals),
        name="flip",
    )(basis)


def invert(dims, meta, place):
    _, _, act, nact = dims
    for a in range(act):
        place[a] = -1
    for i in range(nact):
        place[meta[HEAD + i]] = i


def tile_of(columns, cases):
    half = columns // 2
    return half if cases <= 4 and half % BLOCK == 0 else 2 * BLOCK


def density_kernel(dims, k, h, tile, last, meta, *refs):
    _, n_pts, act, nact = dims
    height = refs[0].shape[0]
    each = act // n_pts
    parts, flipped, before, after, place, table, left = refs[:n_pts], *refs[n_pts:]
    invert(dims, meta, place)
    points = flipped.shape[1]
    rows = []
    left[...] = jnp.zeros_like(left)
    for o in range(n_pts):
        column = meta[1] ^ o
        row = ranked_row(active_rows(dims, meta, 0, column), each - 1 - k, True)
        list_slots(dims, meta, table, o * (nact + 1), 0, column, jnp.maximum(row, 0), True, True)
        rows.append((jnp.maximum(place[column * each + jnp.maximum(row, 0)], 0), row >= 0))
        for slot in range(slots_in(dims, k)):
            j = table[o * (nact + 1) + slot]
            left[o * height : (o + 1) * height, lanes(j)] = parts[o][:, slot * BLOCK : (slot + 1) * BLOCK]

    @pl.loop(0, points // tile)
    def _(t):
        at = pl.ds(pl.multiple_of(t * tile, tile), tile)
        inner = jnp.dot(left[...], flipped[:, at], preferred_element_type=jnp.float32)
        total = before[:, at]
        for o, (spot, valid) in enumerate(rows):
            where = pl.ds(pl.multiple_of(spot * BLOCK + h * height, height), height)
            own = flipped[where, at].astype(jnp.float32)
            share = jnp.sum(inner[o * height : (o + 1) * height] * own, axis=0, keepdims=True)
            total = total + jnp.where(valid, share, jnp.zeros_like(share))
        if last:
            point = t * tile + lax.broadcasted_iota(jnp.int32, total.shape, 1)
            total = jnp.where(point < meta[2], total, jnp.zeros_like(total))
        after[:, at] = total


def density(dims, k, h, meta, parts, flipped, before):
    _, n_pts, act, nact = dims
    orbitals, points = flipped.shape
    height = parts[0].shape[0]
    return pl.pallas_call(
        functools.partial(density_kernel, dims, k, h, tile_of(points, n_pts), False),
        out_shape=jax.ShapeDtypeStruct((1, points), jnp.float32),
        in_specs=[pl.BlockSpec(memory_space=pltpu.SMEM)] + [VM] * (n_pts + 2),
        out_specs=VM,
        scratch_shapes=[
            pltpu.SMEM((act,), jnp.int32),
            pltpu.SMEM((n_pts * (nact + 1),), jnp.int32),
            pltpu.VMEM((n_pts * height, orbitals), jnp.bfloat16),
        ],
        compiler_params=GRANT,
        cost_estimate=cost(2 * n_pts * height * orbitals * points, 2 * orbitals * points),
    )(meta, *parts, flipped, before)


def turn_kernel(dims, k, h, tile, meta, *refs):
    _, n_pts, _, _ = dims
    parts, (flipped, before, basis, kern, pert, weight) = refs[:n_pts], refs[n_pts : n_pts + 6]
    out, (n, n_again, place, table, short, left, right) = refs[n_pts + 6 : -7], refs[-7:]
    density_kernel(dims, k, h, tile, True, meta, *parts, flipped, before, n, place, table, short)
    n_again[...] = n[...]
    response_kernel(dims, (0,), tile, meta, flipped, basis, n, kern, pert, weight, *out, place, table, left, right)


def turn(dims, k, h, meta, parts, flipped, before, basis, kern, pert, weight):
    _, n_pts, act, nact = dims
    orbitals, points = flipped.shape
    height = parts[0].shape[0]
    shapes = [jax.ShapeDtypeStruct((BLOCK, slots_out(dims, 0) * BLOCK), jnp.bfloat16)] * n_pts
    shapes += [jax.ShapeDtypeStruct((1, points), jnp.float32)] * 2
    out = pl.pallas_call(
        functools.partial(turn_kernel, dims, k, h, tile_of(points, n_pts)),
        out_shape=shapes,
        in_specs=[pl.BlockSpec(memory_space=pltpu.SMEM)] + [VM] * (n_pts + 6),
        out_specs=[VM] * len(shapes),
        scratch_shapes=[
            pltpu.SMEM((act,), jnp.int32),
            pltpu.SMEM((n_pts * (nact + 1),), jnp.int32),
            pltpu.VMEM((n_pts * height, orbitals), jnp.bfloat16),
            pltpu.VMEM((n_pts * BLOCK, points), jnp.bfloat16),
            pltpu.VMEM((n_pts * BLOCK, orbitals), jnp.bfloat16),
        ],
        compiler_params=pltpu.CompilerParams(vmem_limit_bytes=26 << 20),
        cost_estimate=cost(2 * n_pts * (BLOCK + height) * orbitals * points, 4 * orbitals * points),
        name="turn",
    )(meta, *parts, flipped, before, basis, kern, pert, weight)
    return out[:n_pts], out[-2], out[-1]


def response_kernel(dims, ranks, tile, meta, *refs):
    _, n_pts, act, nact = dims
    each = act // n_pts
    flipped, basis, n, kern, pert, weight = refs[:6]
    out, (place, table, left, right) = refs[6:-4], refs[-4:]
    invert(dims, meta, place)
    points = flipped.shape[1]
    inside = lax.broadcasted_iota(jnp.int32, (1, points), 1) < meta[2]
    scaling = jnp.where(inside, weight[...] * (pert[...] - kern[...] * n[...]), 0.0)
    cases = [(k, o) for k in ranks for o in range(n_pts)]
    for at, (k, o) in enumerate(cases):
        column = meta[1] ^ o
        row = ranked_row(active_rows(dims, meta, 0, column), k, False)
        list_slots(dims, meta, table, at * (nact + 1), 0, column, jnp.maximum(row, 0), False, True)
        spot = jnp.maximum(place[column * each + jnp.maximum(row, 0)], 0)
        own = flipped[rows_at(spot), :].astype(jnp.float32)
        left[at * BLOCK : (at + 1) * BLOCK, :] = jnp.where(row >= 0, own * scaling, 0.0).astype(jnp.bfloat16)

    @pl.loop(0, basis.shape[1] // tile)
    def _(t):
        cols = pl.ds(pl.multiple_of(t * tile, tile), tile)
        right[:, cols] = jnp.dot(left[...], basis[:, cols], preferred_element_type=jnp.float32).astype(jnp.bfloat16)

    for at, (k, o) in enumerate(cases):
        for slot in range(slots_out(dims, k)):
            j = table[at * (nact + 1) + slot]
            out[at][:, slot * BLOCK : (slot + 1) * BLOCK] = right[at * BLOCK : (at + 1) * BLOCK, lanes(j)]


def response(dims, ranks, meta, flipped, basis, n, kern, pert, weight):
    _, n_pts, act, nact = dims
    orbitals, points = flipped.shape
    cases = n_pts * len(ranks)
    shapes = [
        jax.ShapeDtypeStruct((BLOCK, slots_out(dims, k) * BLOCK), jnp.bfloat16) for k in ranks for _ in range(n_pts)
    ]
    out = pl.pallas_call(
        functools.partial(response_kernel, dims, ranks, tile_of(orbitals, cases)),
        out_shape=shapes,
        in_specs=[pl.BlockSpec(memory_space=pltpu.SMEM)] + [VM] * 6,
        out_specs=[VM] * len(shapes),
        scratch_shapes=[
            pltpu.SMEM((act,), jnp.int32),
            pltpu.SMEM((cases * (nact + 1),), jnp.int32),
            pltpu.VMEM((cases * BLOCK, points), jnp.bfloat16),
            pltpu.VMEM((cases * BLOCK, orbitals), jnp.bfloat16),
        ],
        compiler_params=pltpu.CompilerParams(vmem_limit_bytes=26 << 20),
        cost_estimate=cost(2 * cases * BLOCK * orbitals * points, 4 * orbitals * points),
    )(meta, flipped, basis, n, kern, pert, weight)
    return [out[at * n_pts : (at + 1) * n_pts] for at in range(len(ranks))]


def combine_kernel(dims, k, meta, *refs):
    n_mat, n_pts, act, nact = dims
    each = act // n_pts
    strips, before = refs[: (k + 1) * n_pts], refs[(k + 1) * n_pts : (k + 1) * n_pts + k]
    final = k == each - 1
    out, (total, table, held, sem) = refs[(k + 1) * n_pts + k : -4], refs[-4:]
    inner = None if final else out[-1]
    me_pts = meta[1]
    first = me_pts * each
    ranks = []
    for o in range(n_pts):
        flags = active_rows(dims, meta, o, me_pts)
        ranks.append(jnp.where(flags[k] != 0, sum(flags[:k], jnp.int32(0)), -1))
        for i in range(k + 1):

            @pl.when(ranks[o] == i)
            def _(o=o, i=i):
                filled = slots_out(dims, i) * BLOCK
                pltpu.make_async_copy(strips[i * n_pts + o], held.at[o, :, :filled], sem.at[o]).start()

        list_slots(dims, meta, table, o * (nact + 1), o, me_pts, jnp.int32(k), False, False)
    total[...] = jnp.zeros_like(total)
    for o in range(n_pts):
        for i in range(k + 1):

            @pl.when(ranks[o] == i)
            def _(o=o, i=i):
                filled = slots_out(dims, i) * BLOCK
                pltpu.make_async_copy(strips[i * n_pts + o], held.at[o, :, :filled], sem.at[o]).wait()
                for slot in range(slots_out(dims, i)):
                    b = table[o * (nact + 1) + slot]
                    part = held[o, :, slot * BLOCK : (slot + 1) * BLOCK].astype(jnp.float32)
                    total[:, lanes(b)] += part

    for r in range(k):
        total[:, lanes(first + r)] = before[r][:, k * BLOCK : (k + 1) * BLOCK].T
    for r in range(k + 1, each):
        inner[:, r * BLOCK : (r + 1) * BLOCK] = total[:, lanes(first + r)]
    width = act // n_mat
    pattern_at = HEAD + n_pts * nact + (first + k) * act
    for d in range(n_mat):
        for c in range(width):
            b = (meta[0] ^ d) * width + c
            value = total[:, lanes(b)]
            value = jnp.where(meta[pattern_at + b] != 0, value, jnp.zeros_like(value))
            out[d][:, c * BLOCK : (c + 1) * BLOCK] = value.astype(jnp.bfloat16)


def combine(dims, k, meta, strips, before):
    n_mat, n_pts, act, nact = dims
    shapes = [jax.ShapeDtypeStruct((BLOCK, act // n_mat * BLOCK), jnp.bfloat16)] * n_mat
    if k < act // n_pts - 1:
        shapes += [jax.ShapeDtypeStruct((BLOCK, act // n_pts * BLOCK), jnp.float32)]
    given = sum(strips, [])
    out = pl.pallas_call(
        functools.partial(combine_kernel, dims, k),
        out_shape=shapes,
        in_specs=[pl.BlockSpec(memory_space=pltpu.SMEM)] + [ANY] * len(given) + [VM] * k,
        out_specs=[VM] * len(shapes),
        scratch_shapes=[
            pltpu.VMEM((BLOCK, act * BLOCK), jnp.float32),
            pltpu.SMEM((n_pts * (nact + 1),), jnp.int32),
            pltpu.VMEM((n_pts, BLOCK, nact * BLOCK), jnp.bfloat16),
            pltpu.SemaphoreType.DMA((n_pts,)),
        ],
        compiler_params=GRANT,
        cost_estimate=cost(0, 2 * BLOCK * BLOCK * (act + n_pts * nact)),
    )(meta, *given, *before)
    return out[:n_mat], out[n_mat:]


def widen_kernel(n_mat, meta, *refs):
    out = refs[-1]
    for d in range(n_mat):
        out[meta[0] ^ d] = refs[d][...].astype(jnp.float32)


def widen(dims, start, rows, all_rows, meta, given, held):
    n_mat, _, act, _ = dims
    width = act // n_mat * BLOCK
    more = [] if held is None else [held]
    return pl.pallas_call(
        functools.partial(widen_kernel, n_mat),
        out_shape=jax.ShapeDtypeStruct((n_mat, all_rows, width), jnp.float32),
        grid_spec=pltpu.PrefetchScalarGridSpec(
            num_scalar_prefetch=1,
            grid=(1,),
            in_specs=[pl.BlockSpec((rows, width), lambda i, meta: (0, 0))] * n_mat + [ANY] * len(more),
            out_specs=pl.BlockSpec((n_mat, rows, width), lambda i, meta: (0, start // rows, 0)),
        ),
        input_output_aliases={} if held is None else {1 + n_mat: 0},
        compiler_params=GRANT,
        cost_estimate=cost(0, 6 * rows * n_mat * width),
    )(meta, *given, *more)


def pieces_of(k, row_blocks):
    return 2 if k == row_blocks - 1 else 1


def body(dens_blocks, basis_values, kernel, perturbation, quad_weight, point_count, active_blocks, block_pattern):
    n_mat, n_pts = lax.axis_size("mat"), lax.axis_size("pts")
    act, nact = block_pattern.shape[1], active_blocks.shape[2]
    dims = (n_mat, n_pts, act, nact)
    row_blocks = act // n_pts
    me_mat, me_pts = lax.axis_index("mat"), lax.axis_index("pts")

    def to_peer(value, o):
        return lax.ppermute(value, "pts", [(i, i ^ o) for i in range(n_pts)])

    points = basis_values.shape[1]
    basis = basis_values[0]
    own_active = active_blocks[0, 0]

    def across(values):
        out = [values[0]] + [None] * (n_mat - 1)
        for d in range(n_mat - 1, 0, -1):
            out[d] = lax.ppermute(values[d], "mat", [(i, i ^ d) for i in range(n_mat)])
        return out

    arrived = []
    for k in range(row_blocks):
        cut = [
            lax.dynamic_slice(dens_blocks, (me_mat ^ d, k * BLOCK, 0), (1, BLOCK, dens_blocks.shape[2]))[0]
            for d in range(n_mat)
        ]
        arrived.append(across(cut))

    peers = [own_active] + [to_peer(own_active, o) for o in range(1, n_pts)]
    pattern = lax.dynamic_index_in_dim(block_pattern, me_mat, 0, keepdims=False).reshape(-1)
    head = jnp.stack([me_mat, me_pts, point_count[0, 0]]).astype(jnp.int32)
    meta = jnp.concatenate([head] + peers + [pattern])

    flipped = transposed(pltpu.with_memory_space_constraint(basis, pltpu.HBM))

    parts, stages = [], []
    for k in range(row_blocks):
        held, packed = pack(dims, k, pieces_of(k, row_blocks), meta, arrived[k], stages)
        stages.append(held)
        for h, piece in enumerate(packed):
            parts.append((k, h, [piece[0]] + [to_peer(piece[o], o) for o in range(1, n_pts)]))

    n = jnp.zeros((1, points), jnp.float32)
    for k, h, piece in parts[:-1]:
        n = density(dims, k, h, meta, piece, flipped, n)
    k, h, piece = parts[-1]
    sent, n, n_response = turn(dims, k, h, meta, piece, flipped, n, basis, kernel, perturbation, quad_weight)
    emitted = [sent]

    strips = []
    for k in range(row_blocks):
        if k == 1:
            later = tuple(range(1, row_blocks))
            emitted += response(dims, later, meta, flipped, basis, n, kernel, perturbation, quad_weight)
        strips.append([emitted[k][0]] + [to_peer(emitted[k][o], o) for o in range(1, n_pts)])

    inner, result = [], None
    for k in range(row_blocks):
        cut, pairs = combine(dims, k, meta, strips[: k + 1], inner)
        inner += pairs
        back = across(cut)
        result = widen(dims, k * BLOCK, BLOCK, dens_blocks.shape[1], meta, back, result)
    return result, n_response


def solution(mesh):
    placed = (
        P(None, "pts", "mat"),
        P("mat", "pts", None),
        P("mat", "pts"),
        P("mat", "pts"),
        P("mat", "pts"),
        P("mat", "pts"),
        P("mat", "pts", None),
        P(),
    )

    return jax.shard_map(
        body,
        mesh=mesh,
        in_specs=placed,
        out_specs=(P(None, "pts", "mat"), P("mat", "pts")),
        check_vma=False,
    )
```
